256 devices in a mesh: band: 8 (over y, z_hi), domain: 32 (over z_lo, x, core).
Axes of the slice: x: 4, y: 4, z: 8 (z_hi: 2, z_lo: 4; z = z_hi * 4 + z_lo), core: 2. Of those that a mesh axis runs over, the one named last changes fastest.
Arguments:
- orbital_block: bfloat16 [256, 384, 16, 128], P('band', 'domain'), may hold values from -8 to 8
- block_scale: float32 [256, 384], P('band', 'domain'), may hold values from 0.5 to 6
- potential: float32 [384, 16, 128], P('domain'), may hold values from -4 to 0
Outputs:
- orthonormal: bfloat16 [256, 384, 16, 128], P('band', 'domain')
The draws below stay inside these ranges and needn't reach their ends.
All inputs are finite; a program needn't handle non-finite values.
Results may differ from the reference program's by a relative error of at most 0.015.
Values may be sent and summed in bfloat16 or wider, within the bound.
A program may use at most 64 MiB of HBM per device.

```python
import math
import jax
import jax.numpy as jnp
from jax import lax

NBANDS = 256
CX = 12
NY = 16
NZ = 128
NX = 384


def draw_orbital_block(key, part):
    fields = jnp.clip(jax.random.normal(key, (NBANDS + 1, NX, NY, NZ), jnp.float32), -4.0, 4.0)
    mixed = fields[:NBANDS] + 0.5 * fields[1:]
    return mixed.astype(jnp.bfloat16)


def draw_block_scale(key, part):
    slab_count = NX // CX
    heavy_slab = jax.random.randint(jax.random.fold_in(key, 11), (), 0, slab_count)
    plane_slab = lax.broadcasted_iota(jnp.int32, (NBANDS, NX), 1) // CX
    heavy = plane_slab == heavy_slab
    draw_key = jax.random.fold_in(key, 23)
    unit = jax.random.uniform(draw_key, (NBANDS, NX), jnp.float32, 0.0, 1.0)
    background = jnp.exp(math.log(0.5) + unit * math.log(1.4))
    loud = jnp.exp(math.log(4.0) + unit * math.log(1.5))
    return jnp.where(heavy, loud, background)


def level_of(own_key, shape, cuts, smallest, high):
    loudness, own = 1.0, jax.random.fold_in(own_key, 6)
    for position, shards_of in cuts:
        draws = jnp.exp(jax.random.uniform(jax.random.fold_in(own, position), (shards_of,), jnp.float32, smallest / len(cuts), high / len(cuts)))
        loudness = loudness * jnp.repeat(draws, shape[position] // shards_of).reshape([-1 if axis == position else 1 for axis in range(len(shape))])
    return loudness


def setup_inputs(seed: int = 0) -> dict:
    splits = jax.random.split(jax.random.key(seed), 4)
    orbital_block = draw_orbital_block(jax.random.fold_in(splits[3], 71), 0)
    block_scale = draw_block_scale(jax.random.fold_in(splits[3], 71), 0)
    potential = jnp.clip(-4.0 + 4.0 * jax.random.uniform(splits[2], (NX, NY, NZ), jnp.float32) ** level_of(splits[2], (NX, NY, NZ), ((0, 32),), -0.2, 0.2), -4.0, 0.0)
    return dict(orbital_block=orbital_block, block_scale=block_scale, potential=potential)


grid_step = 0.5
stencil_coef = (-5369.0 / 1800.0, 12.0 / 7.0, -15.0 / 56.0, 10.0 / 189.0, -1.0 / 112.0, 2.0 / 1925.0, -1.0 / 16632.0)
lower_end = -4.0
cut_energy = 6.0
upper_end = 43.0

def filter_terms():
    width_e = (upper_end - cut_energy) / 2.0
    centre = (upper_end + cut_energy) / 2.0
    sigma_one = width_e / (lower_end - centre)
    gamma_term = 2.0 / sigma_one
    sigma_two = 1.0 / (gamma_term - sigma_one)
    sigma_three = 1.0 / (gamma_term - sigma_two)
    return (width_e, centre, sigma_one, sigma_two, sigma_three)

def hamiltonian(padded, potential):
    count_x = padded.shape[1] - 12
    count_y = padded.shape[2] - 12
    count_z = padded.shape[3] - 12

    def window(shift_x, shift_y, shift_z):
        return padded[:, 6 + shift_x:6 + shift_x + count_x, 6 + shift_y:6 + shift_y + count_y, 6 + shift_z:6 + shift_z + count_z].astype(jnp.float32)
    kinetic = -0.5 / (grid_step * grid_step)
    result = (3.0 * stencil_coef[0] * kinetic + potential[None]) * window(0, 0, 0)
    for offset in range(1, 7):
        neighbours = window(offset, 0, 0) + window(-offset, 0, 0) + window(0, offset, 0) + window(0, -offset, 0) + window(0, 0, offset) + window(0, 0, -offset)
        result = result + kinetic * stencil_coef[offset] * neighbours
    return result

def filter_group(orbitals, scales, potential):
    scaled = (orbitals.astype(jnp.float32) * scales[:, :, None, None]).astype(jnp.bfloat16)
    width_e, centre, sigma_one, sigma_two, sigma_three = filter_terms()

    def shifted(source_field):
        padded = jnp.pad(source_field, ((0, 0), (6, 6), (6, 6), (6, 6)))
        return hamiltonian(padded, potential) - centre * source_field.astype(jnp.float32)
    first_iter = (shifted(scaled) * (sigma_one / width_e)).astype(jnp.bfloat16)
    second = (2.0 * sigma_two / width_e * shifted(first_iter) - sigma_one * sigma_two * scaled.astype(jnp.float32)).astype(jnp.bfloat16)
    third_iter = (2.0 * sigma_three / width_e * shifted(second) - sigma_two * sigma_three * first_iter.astype(jnp.float32)).astype(jnp.bfloat16)
    return third_iter

def reference(orbital_block, block_scale, potential):
    group_rows = min(32, NBANDS)
    blocks = orbital_block.reshape(NBANDS // group_rows, group_rows, NX, NY, NZ)
    scale_blocks = block_scale.reshape(NBANDS // group_rows, group_rows, NX)
    filtered = lax.map(lambda pieces: filter_group(pieces[0], pieces[1], potential), (blocks, scale_blocks))
    filtered = filtered.reshape(NBANDS, NX, NY * NZ)

    def add_plane(plane_index, gram_sum):
        plane_rows = lax.dynamic_index_in_dim(filtered, plane_index, 1, keepdims=False)
        return gram_sum + lax.dot_general(plane_rows.astype(jnp.float32), plane_rows.astype(jnp.float32), (((1,), (1,)), ((), ())), preferred_element_type=jnp.float32)
    gram_sum = lax.fori_loop(0, NX, add_plane, jnp.zeros((NBANDS, NBANDS), jnp.float32))
    correlation = gram_sum / float(NX * NY * NZ)
    lower_factor = jnp.linalg.cholesky(correlation)
    inverse = jax.scipy.linalg.solve_triangular(lower_factor, jnp.eye(NBANDS, dtype=jnp.float32), lower=True)
    rotation = inverse.astype(jnp.bfloat16)

    def rotate_plane(plane_index, rotated):
        plane_rows = lax.dynamic_index_in_dim(filtered, plane_index, 1, keepdims=False)
        mixed = jnp.dot(rotation.astype(jnp.float32), plane_rows.astype(jnp.float32), preferred_element_type=jnp.float32).astype(jnp.bfloat16)
        return lax.dynamic_update_index_in_dim(rotated, mixed, plane_index, 1)
    rotated = lax.fori_loop(0, NX, rotate_plane, jnp.zeros((NBANDS, NX, NY * NZ), jnp.bfloat16))
    return rotated.reshape(NBANDS, NX, NY, NZ)
```

```python
import functools
import jax
import jax.numpy as jnp
from jax import lax
from jax.experimental import pallas as pl
from jax.experimental.pallas import tpu as pltpu
from jax.sharding import PartitionSpec as P

MESH = pl.DeviceIdType.MESH


def remote(src, dst, send_sem, recv_sem, device):
    return pltpu.make_async_remote_copy(
        src_ref=src, dst_ref=dst, send_sem=send_sem, recv_sem=recv_sem,
        device_id=device, device_id_type=MESH,
    )


def all_reduce_kernel(nx, ny, nzl, nzh, part_ref, out_ref, half, rows, line, mine,
                      core_s, core_r, plane_s, plane_r, line_s, line_r, back_s, back_r, last_s, last_r):
    band = lax.axis_index("band")
    domain = lax.axis_index("domain")
    y, z_hi = band // nzh, lax.rem(band, nzh)
    core = lax.rem(domain, 2)
    x = lax.rem(domain // 2, nx)
    z_lo = domain // (2 * nx)
    place = y * nx + x
    planes = nx * ny
    level = z_hi * nzl + z_lo
    levels = nzl * nzh
    size = part_ref.shape[0]
    halfrows = size // 2
    piece = halfrows // planes

    partner = (band, domain + 1 - 2 * core)

    def at_place(p):
        return ((p // nx) * nzh + z_hi, (z_lo * nx + lax.rem(p, nx)) * 2 + core)

    def at_level(l):
        return (y * nzh + l // nzl, (lax.rem(l, nzl) * nx + x) * 2 + core)

    barrier = pltpu.get_barrier_semaphore()
    pl.semaphore_signal(barrier, inc=1, device_id=partner, device_id_type=MESH)
    for k in range(1, planes):
        pl.semaphore_signal(barrier, inc=1, device_id=at_place(lax.rem(place + k, planes)), device_id_type=MESH)
    for k in range(1, levels):
        pl.semaphore_signal(barrier, inc=1, device_id=at_level(lax.rem(level + k, levels)), device_id_type=MESH)
    pl.semaphore_wait(barrier, planes + levels - 1)

    mine_at = pl.multiple_of(core * halfrows, 8)
    other_at = pl.multiple_of((1 - core) * halfrows, 8)
    swap = remote(part_ref.at[pl.ds(other_at, halfrows)], half, core_s, core_r, partner)
    swap.start()
    swap.wait()
    half[...] += part_ref[pl.ds(mine_at, halfrows), :]

    copies = []
    for k in range(1, planes):
        p = lax.rem(place + k, planes)
        copy = remote(half.at[pl.ds(pl.multiple_of(p * piece, 8), piece)], rows.at[place],
                      plane_s.at[k], plane_r.at[k], at_place(p))
        copy.start()
        copies.append(copy)
    rows[place] = half[pl.ds(pl.multiple_of(place * piece, 8), piece), :]
    for copy in copies:
        copy.wait()
    total = rows[0]
    for k in range(1, planes):
        total = total + rows[k]
    mine[...] = total

    copies = []
    for k in range(1, levels):
        l = lax.rem(level + k, levels)
        copy = remote(mine, line.at[level], line_s.at[k], line_r.at[k], at_level(l))
        copy.start()
        copies.append(copy)
    line[level] = mine[...]
    for copy in copies:
        copy.wait()
    total = line[0]
    for k in range(1, levels):
        total = total + line[k]
    own = pl.ds(pl.multiple_of(mine_at + place * piece, 8), piece)
    out_ref[own, :] = total

    copies = []
    for k in range(1, planes):
        p = lax.rem(place + k, planes)
        copy = remote(out_ref.at[own], out_ref.at[own], back_s.at[k], back_r.at[k], at_place(p))
        copy.start()
        copies.append(copy)
    for copy in copies:
        copy.wait()
    span = pl.ds(mine_at, halfrows)
    final = remote(out_ref.at[span], out_ref.at[span], last_s, last_r, partner)
    final.start()
    final.wait()


def all_reduce(part, nx, ny, nzl, nzh, collective_id):
    size, width = part.shape
    planes, levels = nx * ny, nzl * nzh
    piece = size // 2 // planes
    dma = pltpu.SemaphoreType.DMA
    f32 = jnp.float32
    return pl.pallas_call(
        functools.partial(all_reduce_kernel, nx, ny, nzl, nzh),
        out_shape=jax.ShapeDtypeStruct((size, width), f32),
        in_specs=[pl.BlockSpec(memory_space=pltpu.VMEM)],
        out_specs=pl.BlockSpec(memory_space=pltpu.VMEM),
        scratch_shapes=[
            pltpu.VMEM((size // 2, width), f32),
            pltpu.VMEM((planes, piece, width), f32),
            pltpu.VMEM((levels, piece, width), f32),
            pltpu.VMEM((piece, width), f32),
            dma, dma, dma((planes,)), dma((planes,)), dma((levels,)), dma((levels,)),
            dma((planes,)), dma((planes,)), dma, dma,
        ],
        compiler_params=pltpu.CompilerParams(collective_id=collective_id, has_side_effects=True),
        name="correlation_sum",
    )(part)

grid_step = 0.5
stencil_coef = (
    -5369.0 / 1800.0,
    12.0 / 7.0,
    -15.0 / 56.0,
    10.0 / 189.0,
    -1.0 / 112.0,
    2.0 / 1925.0,
    -1.0 / 16632.0,
)
lower_end = -4.0
cut_energy = 6.0
upper_end = 43.0


def padded_2(block, sides, width):
    for axis, dim in sides:
        count = lax.axis_size(axis)
        forward = [(i, i + 1) for i in range(count - 1)]
        backward = [(target, source) for source, target in forward]
        low = lax.ppermute(
            lax.slice_in_dim(block, block.shape[dim] - width, None, axis=dim), axis, forward
        )
        high = lax.ppermute(lax.slice_in_dim(block, 0, width, axis=dim), axis, backward)
        block = jnp.concatenate([low, block, high], axis=dim)
    return block


def filter_terms():
    width_e = (upper_end - cut_energy) / 2.0
    centre = (upper_end + cut_energy) / 2.0
    sigma_one = width_e / (lower_end - centre)
    gamma_term = 2.0 / sigma_one
    sigma_two = 1.0 / (gamma_term - sigma_one)
    sigma_three = 1.0 / (gamma_term - sigma_two)
    return (width_e, centre, sigma_one, sigma_two, sigma_three)


def hamiltonian(padded, potential):
    count_x = padded.shape[1] - 12
    count_y = padded.shape[2] - 12
    count_z = padded.shape[3] - 12

    def window(shift_x, shift_y, shift_z):
        return padded[
            :,
            6 + shift_x : 6 + shift_x + count_x,
            6 + shift_y : 6 + shift_y + count_y,
            6 + shift_z : 6 + shift_z + count_z,
        ].astype(jnp.float32)

    kinetic = -0.5 / (grid_step * grid_step)
    result = (3.0 * stencil_coef[0] * kinetic + potential[None]) * window(0, 0, 0)
    for offset in range(1, 7):
        neighbours = (
            window(offset, 0, 0)
            + window(-offset, 0, 0)
            + window(0, offset, 0)
            + window(0, -offset, 0)
            + window(0, 0, offset)
            + window(0, 0, -offset)
        )
        result = result + kinetic * stencil_coef[offset] * neighbours
    return result


def body(orbital_block, block_scale, potential):
    band_rows, planes, rows_y, rows_z = orbital_block.shape
    width_e, centre, sigma_one, sigma_two, sigma_three = filter_terms()
    scaled = (orbital_block.astype(jnp.float32) * block_scale[:, :, None, None]).astype(
        jnp.bfloat16
    )

    def centred(extended, energies):
        padded = jnp.pad(extended, ((0, 0), (0, 0), (6, 6), (6, 6)))
        middle = extended[:, 6 : extended.shape[1] - 6].astype(jnp.float32)
        return hamiltonian(padded, energies) - centre * middle

    def extend(source_field):
        return padded_2(source_field, (("domain", 1),), 6)

    first_iter = (centred(extend(scaled), potential) * (sigma_one / width_e)).astype(jnp.bfloat16)
    second = (
        2.0 * sigma_two / width_e * centred(extend(first_iter), potential)
        - sigma_one * sigma_two * scaled.astype(jnp.float32)
    ).astype(jnp.bfloat16)
    third_iter = (
        2.0 * sigma_three / width_e * centred(extend(second), potential)
        - sigma_two * sigma_three * first_iter.astype(jnp.float32)
    ).astype(jnp.bfloat16)
    cell_count = planes * rows_y * rows_z
    flattened = third_iter.reshape(band_rows, cell_count)
    columns = lax.all_to_all(flattened, "band", split_axis=1, concat_axis=0, tiled=True)
    partial_gram = lax.dot_general(
        columns, columns, (((1,), (1,)), ((), ())), preferred_element_type=jnp.float32
    )
    gram_sum = all_reduce(partial_gram, 4, 4, 4, 2, 1)
    correlation = gram_sum / float(cell_count * lax.axis_size("domain"))
    lower_factor = jnp.linalg.cholesky(correlation)
    inverse = jax.scipy.linalg.solve_triangular(
        lower_factor, jnp.eye(correlation.shape[0], dtype=jnp.float32), lower=True
    )
    rotation = inverse.astype(jnp.bfloat16)
    mixed = jnp.dot(rotation, columns, preferred_element_type=jnp.float32).astype(jnp.bfloat16)
    returned = lax.all_to_all(mixed, "band", split_axis=0, concat_axis=1, tiled=True)
    return returned.reshape(band_rows, planes, rows_y, rows_z)


def solution(mesh):
    in_specs = (P("band", "domain", None, None), P("band", "domain"), P("domain", None, None))
    out_specs = P("band", "domain", None, None)
    return jax.shard_map(body, mesh=mesh, in_specs=in_specs, out_specs=out_specs, check_vma=False)
```

```python
import functools

import jax
import jax.numpy as jnp
import ml_dtypes
import numpy as np
from jax import lax
from jax.experimental import pallas as pl
from jax.experimental.pallas import tpu as pltpu
from jax.sharding import PartitionSpec as P

MESH = pl.DeviceIdType.MESH

grid_step = 0.5
stencil_coef = (
    -5369.0 / 1800.0,
    12.0 / 7.0,
    -15.0 / 56.0,
    10.0 / 189.0,
    -1.0 / 112.0,
    2.0 / 1925.0,
    -1.0 / 16632.0,
)
lower_end = -4.0
cut_energy = 6.0
upper_end = 43.0


def filter_terms():
    width_e = (upper_end - cut_energy) / 2.0
    centre = (upper_end + cut_energy) / 2.0
    sigma_one = width_e / (lower_end - centre)
    gamma_term = 2.0 / sigma_one
    sigma_two = 1.0 / (gamma_term - sigma_one)
    sigma_three = 1.0 / (gamma_term - sigma_two)
    return (width_e, centre, sigma_one, sigma_two, sigma_three)


def remote(src, dst, send_sem, recv_sem, device):
    return pltpu.make_async_remote_copy(
        src_ref=src, dst_ref=dst, send_sem=send_sem, recv_sem=recv_sem,
        device_id=device, device_id_type=MESH,
    )


def all_reduce_kernel(nx, ny, nzl, nzh, part_ref, out_ref, half, rows, line, mine,
                      core_s, core_r, plane_s, plane_r, line_s, line_r, back_s, back_r, last_s, last_r):
    band = lax.axis_index("band")
    domain = lax.axis_index("domain")
    y, z_hi = band // nzh, lax.rem(band, nzh)
    core = lax.rem(domain, 2)
    x = lax.rem(domain // 2, nx)
    z_lo = domain // (2 * nx)
    place = y * nx + x
    planes = nx * ny
    level = z_hi * nzl + z_lo
    levels = nzl * nzh
    size = part_ref.shape[0]
    halfrows = size // 2
    piece = halfrows // planes

    partner = (band, domain + 1 - 2 * core)

    def at_place(p):
        return ((p // nx) * nzh + z_hi, (z_lo * nx + lax.rem(p, nx)) * 2 + core)

    def at_level(l):
        return (y * nzh + l // nzl, (lax.rem(l, nzl) * nx + x) * 2 + core)

    barrier = pltpu.get_barrier_semaphore()
    pl.semaphore_signal(barrier, inc=1, device_id=partner, device_id_type=MESH)
    for k in range(1, planes):
        pl.semaphore_signal(barrier, inc=1, device_id=at_place(lax.rem(place + k, planes)), device_id_type=MESH)
    for k in range(1, levels):
        pl.semaphore_signal(barrier, inc=1, device_id=at_level(lax.rem(level + k, levels)), device_id_type=MESH)
    pl.semaphore_wait(barrier, planes + levels - 1)

    mine_at = pl.multiple_of(core * halfrows, 8)
    other_at = pl.multiple_of((1 - core) * halfrows, 8)
    swap = remote(part_ref.at[pl.ds(other_at, halfrows)], half, core_s, core_r, partner)
    swap.start()
    swap.wait()
    half[...] += part_ref[pl.ds(mine_at, halfrows), :]

    copies = []
    for k in range(1, planes):
        p = lax.rem(place + k, planes)
        copy = remote(half.at[pl.ds(pl.multiple_of(p * piece, 8), piece)], rows.at[place],
                      plane_s.at[k], plane_r.at[k], at_place(p))
        copy.start()
        copies.append(copy)
    rows[place] = half[pl.ds(pl.multiple_of(place * piece, 8), piece), :]
    for copy in copies:
        copy.wait()
    total = rows[0]
    for k in range(1, planes):
        total = total + rows[k]
    mine[...] = total

    copies = []
    for k in range(1, levels):
        l = lax.rem(level + k, levels)
        copy = remote(mine, line.at[level], line_s.at[k], line_r.at[k], at_level(l))
        copy.start()
        copies.append(copy)
    line[level] = mine[...]
    for copy in copies:
        copy.wait()
    total = line[0]
    for k in range(1, levels):
        total = total + line[k]
    own = pl.ds(pl.multiple_of(mine_at + place * piece, 8), piece)
    out_ref[own, :] = total

    copies = []
    for k in range(1, planes):
        p = lax.rem(place + k, planes)
        copy = remote(out_ref.at[own], out_ref.at[own], back_s.at[k], back_r.at[k], at_place(p))
        copy.start()
        copies.append(copy)
    for copy in copies:
        copy.wait()
    span = pl.ds(mine_at, halfrows)
    final = remote(out_ref.at[span], out_ref.at[span], last_s, last_r, partner)
    final.start()
    final.wait()


def all_reduce(part, nx, ny, nzl, nzh, collective_id):
    size, width = part.shape
    planes, levels = nx * ny, nzl * nzh
    piece = size // 2 // planes
    dma = pltpu.SemaphoreType.DMA
    f32 = jnp.float32
    return pl.pallas_call(
        functools.partial(all_reduce_kernel, nx, ny, nzl, nzh),
        out_shape=jax.ShapeDtypeStruct((size, width), f32),
        in_specs=[pl.BlockSpec(memory_space=pltpu.VMEM)],
        out_specs=pl.BlockSpec(memory_space=pltpu.VMEM),
        scratch_shapes=[
            pltpu.VMEM((size // 2, width), f32),
            pltpu.VMEM((planes, piece, width), f32),
            pltpu.VMEM((levels, piece, width), f32),
            pltpu.VMEM((piece, width), f32),
            dma, dma, dma((planes,)), dma((planes,)), dma((levels,)), dma((levels,)),
            dma((planes,)), dma((planes,)), dma, dma,
        ],
        compiler_params=pltpu.CompilerParams(collective_id=collective_id, has_side_effects=True),
        name="correlation_sum",
    )(part)


def rotation_kernel(panel, cells, gram_ref, out_ref, work):
    size = gram_ref.shape[0]
    work[...] = gram_ref[...] * (1.0 / cells)
    lane = lax.broadcasted_iota(jnp.int32, (panel, size), 1)
    row = lax.broadcasted_iota(jnp.int32, (panel, size), 0)
    sub = lax.broadcasted_iota(jnp.int32, (panel, 128), 0)
    wide = lax.broadcasted_iota(jnp.int32, (size, size), 1)

    def step(k, carry):
        start = pl.multiple_of(k * panel, panel)
        tile = pl.multiple_of((start // 128) * 128, 128)
        here = pl.ds(start, panel)
        corner = pltpu.roll(work[here, pl.ds(tile, 128)], 128 - (start - tile), 1)
        rows = work[here, :]
        inside = (lane >= start) & (lane < start + panel)
        rows = jnp.where(inside, jnp.where(lane - start == row, 1.0, 0.0), rows)
        columns = [jnp.broadcast_to(corner[:, j : j + 1], (panel, 128)) for j in range(panel)]
        pivots = jnp.ones((panel, 128), jnp.float32)
        for j in range(panel):
            column = columns[j]
            spread = [jnp.broadcast_to(column[l : l + 1, :], (panel, 128)) for l in range(j, panel)]
            pivot = spread[0]
            pivots = jnp.where(sub == j, pivot, pivots)
            if j < panel - 1:
                factor = jnp.where(sub > j, column * (1.0 / pivot), 0.0)
                for l in range(j + 1, panel):
                    columns[l] = columns[l] - factor * spread[l - j]
                wide_factor = jnp.concatenate([factor] * (size // 128), axis=1)
                rows = rows - wide_factor * jnp.broadcast_to(rows[j : j + 1, :], (panel, size))
        scale = lax.rsqrt(pivots)
        rows = rows * jnp.concatenate([scale] * (size // 128), axis=1)
        below = jnp.where(lane >= start + panel, rows, 0.0)
        change = lax.dot_general(
            below, rows, (((0,), (0,)), ((), ())),
            precision=lax.Precision.HIGHEST, preferred_element_type=jnp.float32,
        )
        keep = (wide >= start) & (wide < start + panel)
        work[...] = jnp.where(keep, 0.0, work[...]) - change
        work[here, :] = rows
        return carry

    lax.fori_loop(0, size // panel, step, 0)
    down = lax.broadcasted_iota(jnp.int32, (size, size), 0)
    out_ref[...] = jnp.where(wide <= down, work[...], 0.0).astype(out_ref.dtype)


def rotation_of(gram, cells, panel=16):
    size = gram.shape[0]
    return pl.pallas_call(
        functools.partial(rotation_kernel, panel, cells),
        out_shape=jax.ShapeDtypeStruct((size, size), jnp.bfloat16),
        in_specs=[pl.BlockSpec(memory_space=pltpu.VMEM)],
        out_specs=pl.BlockSpec(memory_space=pltpu.VMEM),
        scratch_shapes=[pltpu.VMEM((size, size), jnp.float32)],
        name="rotation",
    )(gram)


def stencil_matrices(planes, rows_y, rows_z):
    reach = len(stencil_coef) - 1
    kinetic = -0.5 / (grid_step * grid_step)
    plane_part = np.zeros((planes, rows_y, planes + 2 * reach, rows_y), np.float64)
    line_part = np.zeros((rows_z, rows_z), np.float64)
    for m in range(1, reach + 1):
        weight = kinetic * stencil_coef[m]
        for sign in (-m, m):
            for x in range(planes):
                for y in range(rows_y):
                    plane_part[x, y, x + reach + sign, y] += weight
                    if 0 <= y + sign < rows_y:
                        plane_part[x, y, x + reach, y + sign] += weight
            for z in range(rows_z):
                if 0 <= z + sign < rows_z:
                    line_part[z + sign, z] += weight
    plane_part = plane_part.reshape(planes * rows_y, (planes + 2 * reach) * rows_y)

    def halves(matrix):
        high = matrix.astype(ml_dtypes.bfloat16)
        low = (matrix - high.astype(np.float64)).astype(ml_dtypes.bfloat16)
        return np.concatenate([high, low], axis=0)

    return halves(plane_part), halves(line_part)


GROUP = 8
SHARE = 16


def filter_kernel(
    nb, nd, orb_ref, scale_ref, pot_ref, plane_ref, line_ref, cols_ref, gram_ref,
    ext0, ext1, ext2, full, turned, energy,
    up_s, up_r, down_s, down_r, share_s, share_r,
):
    band = lax.axis_index("band")
    domain = lax.axis_index("domain")
    orbitals, planes, rows_y, rows_z = orb_ref.shape
    reach = len(stencil_coef) - 1
    cells_xy = planes * rows_y
    part = cells_xy // nb
    groups = orbitals // GROUP
    ext = (ext0, ext1, ext2)
    has_low, has_high = domain > 0, domain < nd - 1
    width_e, centre, sigma_one, sigma_two, sigma_three = filter_terms()
    kinetic = -0.5 / (grid_step * grid_step)

    barrier = pltpu.get_barrier_semaphore()

    @pl.when(has_low)
    def _():
        pl.semaphore_signal(barrier, inc=1, device_id=(band, domain - 1), device_id_type=MESH)

    @pl.when(has_high)
    def _():
        pl.semaphore_signal(barrier, inc=1, device_id=(band, domain + 1), device_id_type=MESH)

    for k in range(1, nb):
        pl.semaphore_signal(barrier, inc=1, device_id=(lax.rem(band + k, nb), domain), device_id_type=MESH)

    def scale_group(g):
        def one(i, carry):
            o = g * GROUP + i
            for p in range(planes):
                ext0[o, reach + p] = (orb_ref[o, p].astype(jnp.float32) * scale_ref[o, p]).astype(jnp.bfloat16)
            return carry

        lax.fori_loop(0, GROUP, one, 0)

    def upward(s, g):
        some = pl.ds(g * GROUP, GROUP)
        return remote(ext[s].at[some, pl.ds(planes, reach)], ext[s].at[some, pl.ds(0, reach)],
                      up_s.at[s, g], up_r.at[s, g], (band, domain + 1))

    def downward(s, g):
        some = pl.ds(g * GROUP, GROUP)
        return remote(ext[s].at[some, pl.ds(reach, reach)], ext[s].at[some, pl.ds(planes + reach, reach)],
                      down_s.at[s, g], down_r.at[s, g], (band, domain - 1))

    def send_edges(s, g):
        @pl.when(has_high)
        def _():
            upward(s, g).start()

        @pl.when(has_low)
        def _():
            downward(s, g).start()

    def await_edges(s, g):
        @pl.when(has_low)
        def _():
            upward(s, g).wait_recv()

        @pl.when(has_high)
        def _():
            downward(s, g).wait_recv()

    def apply(s, g):
        def pair(i, carry):
            o = g * GROUP + 2 * i
            sources = [ext[s][o + q].reshape((planes + 2 * reach) * rows_y, rows_z) for q in range(2)]
            both = jnp.concatenate(sources, axis=1)
            spread = jnp.dot(plane_ref[...], both, preferred_element_type=jnp.float32)
            spread = spread[:cells_xy] + spread[cells_xy:]
            first_row = reach * rows_y
            for q in range(2):
                middle = sources[q][first_row : first_row + cells_xy]
                along = jnp.dot(
                    jnp.concatenate([middle, middle], axis=1), line_ref[...], preferred_element_type=jnp.float32
                )
                total = spread[:, q * rows_z : (q + 1) * rows_z] + along + energy[...] * middle.astype(jnp.float32)
                if s == 0:
                    value = total * (sigma_one / width_e)
                else:
                    earlier = ext[s - 1][o + q, pl.ds(reach, planes)].reshape(cells_xy, rows_z).astype(jnp.float32)
                    if s == 1:
                        value = total * (2.0 * sigma_two / width_e) - (sigma_one * sigma_two) * earlier
                    else:
                        value = total * (2.0 * sigma_three / width_e) - (sigma_two * sigma_three) * earlier
                if s < 2:
                    ext[s + 1][o + q, pl.ds(reach, planes)] = value.astype(jnp.bfloat16).reshape(planes, rows_y, rows_z)
                else:
                    full[lax.rem(o, SHARE) + q] = value
            return carry

        lax.fori_loop(0, GROUP // 2, pair, 0)

    def turn(h):
        def block(r, carry):
            at = pl.multiple_of(r * 8, 8)
            piece = full[:, pl.ds(at, 8), :]
            turned[pl.ds(at, 8), pl.ds(h * SHARE, SHARE), :] = jnp.swapaxes(piece, 0, 1).astype(jnp.bfloat16)
            return carry

        lax.fori_loop(0, cells_xy // 8, block, 0)

    def place_of(b, h):
        return pl.ds(pl.multiple_of(b * orbitals + h * SHARE, SHARE), SHARE)

    def share(h, k):
        target = lax.rem(band + k, nb)
        return remote(turned.at[pl.ds(target * part, part), pl.ds(h * SHARE, SHARE)],
                      cols_ref.at[:, place_of(band, h)],
                      share_s.at[h, k], share_r.at[h, k], (target, domain))

    energy[...] = pot_ref[...].reshape(cells_xy, rows_z) + (3.0 * stencil_coef[0] * kinetic - centre)
    scale_group(0)
    pl.semaphore_wait(barrier, nb - 1 + has_low.astype(jnp.int32) + has_high.astype(jnp.int32))

    send_edges(0, 0)
    for g in range(1, groups):
        scale_group(g)
        send_edges(0, g)

    @pl.when(jnp.logical_not(has_low))
    def _():
        for s in range(3):
            ext[s][:, :reach] = jnp.zeros((orbitals, reach, rows_y, rows_z), jnp.bfloat16)

    @pl.when(jnp.logical_not(has_high))
    def _():
        for s in range(3):
            ext[s][:, planes + reach :] = jnp.zeros((orbitals, reach, rows_y, rows_z), jnp.bfloat16)

    for s, g in ((0, 0), (0, 1), (1, 0), (1, 1), (0, 2), (2, 0), (2, 1), (0, 3), (1, 2), (1, 3), (2, 2), (2, 3)):
        await_edges(s, g)
        apply(s, g)
        if s < 2:
            send_edges(s + 1, g)
        elif g % 2 == 1:
            h = g // 2
            turn(h)
            for k in range(1, nb):
                share(h, k).start()
            cols_ref[:, place_of(band, h), :] = turned[pl.ds(band * part, part), pl.ds(h * SHARE, SHARE), :]

    for h in range(orbitals // SHARE):
        for k in range(1, nb):
            share(h, k).wait()

    def gram_step(i, total):
        line = jnp.concatenate([cols_ref[2 * i], cols_ref[2 * i + 1]], axis=1)
        return total + lax.dot_general(line, line, (((1,), (1,)), ((), ())), preferred_element_type=jnp.float32)

    gram_ref[...] = lax.fori_loop(0, part // 2, gram_step, jnp.zeros(gram_ref.shape, jnp.float32))

    for s in range(3):
        for g in range(groups):
            @pl.when(has_high)
            def _():
                upward(s, g).wait_send()

            @pl.when(has_low)
            def _():
                downward(s, g).wait_send()


def filtered_columns(orbital_block, block_scale, potential, nb, nd, collective_id):
    orbitals, planes, rows_y, rows_z = orbital_block.shape
    reach = len(stencil_coef) - 1
    plane_part, line_part = stencil_matrices(planes, rows_y, rows_z)
    cells_xy = planes * rows_y
    groups = orbitals // GROUP
    halves = orbitals // SHARE
    dma = pltpu.SemaphoreType.DMA
    f32, bf16 = jnp.float32, jnp.bfloat16
    vmem = pl.BlockSpec(memory_space=pltpu.VMEM)
    wide = pltpu.VMEM((orbitals, planes + 2 * reach, rows_y, rows_z), bf16)
    return pl.pallas_call(
        functools.partial(filter_kernel, nb, nd),
        out_shape=(
            jax.ShapeDtypeStruct((cells_xy // nb, nb * orbitals, rows_z), bf16),
            jax.ShapeDtypeStruct((nb * orbitals, nb * orbitals), f32),
        ),
        in_specs=[vmem, pl.BlockSpec(memory_space=pltpu.SMEM), vmem, vmem, vmem],
        out_specs=(vmem, vmem),
        scratch_shapes=[
            wide, wide, wide,
            pltpu.VMEM((SHARE, cells_xy, rows_z), f32),
            pltpu.VMEM((cells_xy, orbitals, rows_z), bf16),
            pltpu.VMEM((cells_xy, rows_z), f32),
            dma((3, groups)), dma((3, groups)), dma((3, groups)), dma((3, groups)),
            dma((halves, nb)), dma((halves, nb)),
        ],
        compiler_params=pltpu.CompilerParams(collective_id=collective_id, has_side_effects=True, vmem_limit_bytes=48 << 20),
        name="filter",
    )(orbital_block, block_scale, potential, jnp.asarray(plane_part), jnp.asarray(line_part))


def rotate_kernel(nb, rot_ref, cols_ref, out_ref, mixed, send, recv):
    band = lax.axis_index("band")
    domain = lax.axis_index("domain")
    part, total, rows_z = cols_ref.shape
    orbitals = total // nb
    barrier = pltpu.get_barrier_semaphore()
    for k in range(1, nb):
        pl.semaphore_signal(barrier, inc=1, device_id=(lax.rem(band + k, nb), domain), device_id_type=MESH)

    chunks = send.shape[0]
    span = part // chunks

    def back(c, k):
        target = lax.rem(band + k, nb)
        rows = pl.ds(pl.multiple_of(target * orbitals, orbitals), orbitals)
        return remote(mixed.at[pl.ds(c * span, span), rows],
                      out_ref.at[pl.ds(band * part + c * span, span)],
                      send.at[c, k], recv.at[c, k], (target, domain))

    for c in range(chunks):
        def mix(i, carry):
            r = c * span + 2 * i
            line = jnp.concatenate([cols_ref[r], cols_ref[r + 1]], axis=1)
            value = jnp.dot(rot_ref[...], line, preferred_element_type=jnp.float32).astype(jnp.bfloat16)
            mixed[r] = value[:, :rows_z]
            mixed[r + 1] = value[:, rows_z:]
            return carry

        lax.fori_loop(0, span // 2, mix, 0)
        if c == 0:
            pl.semaphore_wait(barrier, nb - 1)
        for k in range(1, nb):
            back(c, k).start()

    own = pl.ds(pl.multiple_of(band * orbitals, orbitals), orbitals)
    out_ref[pl.ds(band * part, part)] = mixed[:, own, :]
    for c in range(chunks):
        for k in range(1, nb):
            back(c, k).wait()


def rotated(rotation, columns, nb, collective_id, chunks=4):
    part, total, rows_z = columns.shape
    orbitals = total // nb
    dma = pltpu.SemaphoreType.DMA
    vmem = pl.BlockSpec(memory_space=pltpu.VMEM)
    return pl.pallas_call(
        functools.partial(rotate_kernel, nb),
        out_shape=jax.ShapeDtypeStruct((part * nb, orbitals, rows_z), jnp.bfloat16),
        in_specs=[vmem, vmem],
        out_specs=vmem,
        scratch_shapes=[pltpu.VMEM((part, total, rows_z), jnp.bfloat16), dma((chunks, nb)), dma((chunks, nb))],
        compiler_params=pltpu.CompilerParams(collective_id=collective_id, has_side_effects=True, vmem_limit_bytes=48 << 20),
        name="rotate",
    )(rotation, columns)


def solution(mesh):
    nb, nd = mesh.shape["band"], mesh.shape["domain"]

    def body(orbital_block, block_scale, potential):
        orbitals, planes, rows_y, rows_z = orbital_block.shape
        columns, part = filtered_columns(orbital_block, block_scale, potential, nb, nd, 1)
        gram = all_reduce(part, 4, 4, 4, 2, 2)
        rotation = rotation_of(gram, float(planes * rows_y * rows_z * nd), 32)
        back = rotated(rotation, columns, nb, 3)
        return back.transpose(1, 0, 2).reshape(orbitals, planes, rows_y, rows_z)

    in_specs = (P("band", "domain", None, None), P("band", "domain"), P("domain", None, None))
    out_specs = P("band", "domain", None, None)
    return jax.shard_map(body, mesh=mesh, in_specs=in_specs, out_specs=out_specs, check_vma=False)
```

```python
import functools

import jax
import jax.numpy as jnp
import ml_dtypes
import numpy as np
from jax import lax
from jax.experimental import pallas as pl
from jax.experimental.pallas import tpu as pltpu
from jax.sharding import PartitionSpec as P

MESH = pl.DeviceIdType.MESH

grid_step = 0.5
stencil_coef = (
    -5369.0 / 1800.0,
    12.0 / 7.0,
    -15.0 / 56.0,
    10.0 / 189.0,
    -1.0 / 112.0,
    2.0 / 1925.0,
    -1.0 / 16632.0,
)
lower_end = -4.0
cut_energy = 6.0
upper_end = 43.0


def filter_terms():
    width_e = (upper_end - cut_energy) / 2.0
    centre = (upper_end + cut_energy) / 2.0
    sigma_one = width_e / (lower_end - centre)
    gamma_term = 2.0 / sigma_one
    sigma_two = 1.0 / (gamma_term - sigma_one)
    sigma_three = 1.0 / (gamma_term - sigma_two)
    return (width_e, centre, sigma_one, sigma_two, sigma_three)


def remote(src, dst, send_sem, recv_sem, device):
    return pltpu.make_async_remote_copy(
        src_ref=src, dst_ref=dst, send_sem=send_sem, recv_sem=recv_sem,
        device_id=device, device_id_type=MESH,
    )


def stencil_matrices(planes, rows_y, rows_z):
    reach = len(stencil_coef) - 1
    kinetic = -0.5 / (grid_step * grid_step)
    plane_part = np.zeros((planes, rows_y, planes + 2 * reach, rows_y), np.float64)
    line_part = np.zeros((rows_z, rows_z), np.float64)
    for m in range(1, reach + 1):
        weight = kinetic * stencil_coef[m]
        for sign in (-m, m):
            for x in range(planes):
                for y in range(rows_y):
                    plane_part[x, y, x + reach + sign, y] += weight
                    if 0 <= y + sign < rows_y:
                        plane_part[x, y, x + reach, y + sign] += weight
            for z in range(rows_z):
                if 0 <= z + sign < rows_z:
                    line_part[z + sign, z] += weight
    plane_part = plane_part.reshape(planes * rows_y, (planes + 2 * reach) * rows_y)

    def halves(matrix):
        high = matrix.astype(ml_dtypes.bfloat16)
        low = (matrix - high.astype(np.float64)).astype(ml_dtypes.bfloat16)
        return np.concatenate([high, low], axis=0)

    return halves(plane_part), halves(line_part)


GROUP = 4
PACK = 8
LAG = 2
STEPS = 3
CHUNKS = 4
PANEL = 32


def step_kernel(
    nx, ny, nzl, nzh, cells,
    orb_hbm, scale_ref, pot_hbm, plane_hbm, line_hbm, out_ref,
    orb, pot, plane_mat, line_mat, ext0, ext1, ext2, full, turned, cols, energy,
    gram, half, rows, line, mine, work, rot, mixed,
    load_s, const_s, up_s, up_r, down_s, down_r, share_s, share_r,
    core_s, core_r, plane_s, plane_r, line_s, line_r, back_s, back_r, last_s, last_r, home_s, home_r,
):
    nb, nd = ny * nzh, nzl * nx * 2
    band = lax.axis_index("band")
    domain = lax.axis_index("domain")
    orbitals, planes, rows_y, rows_z = orb.shape
    reach = len(stencil_coef) - 1
    cells_xy = planes * rows_y
    part = cells_xy // nb
    groups = orbitals // GROUP
    packs = orbitals // PACK
    ext = (ext0, ext1, ext2)
    has_low, has_high = domain > 0, domain < nd - 1
    width_e, centre, sigma_one, sigma_two, sigma_three = filter_terms()
    kinetic = -0.5 / (grid_step * grid_step)

    y, z_hi = band // nzh, lax.rem(band, nzh)
    core = lax.rem(domain, 2)
    x = lax.rem(domain // 2, nx)
    z_lo = domain // (2 * nx)
    place = y * nx + x
    places = nx * ny
    level = z_hi * nzl + z_lo
    levels = nzl * nzh
    partner = (band, domain + 1 - 2 * core)

    def at_place(p):
        return ((p // nx) * nzh + z_hi, (z_lo * nx + lax.rem(p, nx)) * 2 + core)

    def at_level(l):
        return (y * nzh + l // nzl, (lax.rem(l, nzl) * nx + x) * 2 + core)

    def load(g):
        some = pl.ds(g * GROUP, GROUP)
        return pltpu.make_async_copy(orb_hbm.at[some], orb.at[some], load_s.at[g])

    constants = [
        pltpu.make_async_copy(source, target, const_s.at[i])
        for i, (source, target) in enumerate(((pot_hbm, pot), (plane_hbm, plane_mat), (line_hbm, line_mat)))
    ]
    load(0).start()
    for copy in constants:
        copy.start()
    for g in range(1, groups):
        load(g).start()

    barrier = pltpu.get_barrier_semaphore()

    def greet(device):
        pl.semaphore_signal(barrier, inc=1, device_id=device, device_id_type=MESH)

    @pl.when(has_low)
    def _():
        greet((band, domain - 1))

    @pl.when(has_high)
    def _():
        greet((band, domain + 1))

    for k in range(1, nb):
        greet((lax.rem(band + k, nb), domain))
    greet(partner)
    for k in range(1, places):
        greet(at_place(lax.rem(place + k, places)))
    for k in range(1, levels):
        greet(at_level(lax.rem(level + k, levels)))

    def scale_group(g):
        load(g).wait()

        def one(i, carry):
            o = g * GROUP + i
            for p in range(planes):
                ext0[o, reach + p] = (orb[o, p].astype(jnp.float32) * scale_ref[o, p]).astype(jnp.bfloat16)
            return carry

        lax.fori_loop(0, GROUP, one, 0)

    def upward(s, g):
        some = pl.ds(g * GROUP, GROUP)
        return remote(ext[s].at[some, pl.ds(planes, reach)], ext[s].at[some, pl.ds(0, reach)],
                      up_s.at[s, g], up_r.at[s, g], (band, domain + 1))

    def downward(s, g):
        some = pl.ds(g * GROUP, GROUP)
        return remote(ext[s].at[some, pl.ds(reach, reach)], ext[s].at[some, pl.ds(planes + reach, reach)],
                      down_s.at[s, g], down_r.at[s, g], (band, domain - 1))

    def send_edges(s, g):
        @pl.when(has_high)
        def _():
            upward(s, g).start()

        @pl.when(has_low)
        def _():
            downward(s, g).start()

    def await_edges(s, g):
        @pl.when(has_low)
        def _():
            upward(s, g).wait_recv()

        @pl.when(has_high)
        def _():
            downward(s, g).wait_recv()

    def apply(s, g):
        def pair(i, carry):
            o = g * GROUP + 2 * i
            sources = [ext[s][o + q].reshape((planes + 2 * reach) * rows_y, rows_z) for q in range(2)]
            both = jnp.concatenate(sources, axis=1)
            spread = jnp.dot(plane_mat[...], both, preferred_element_type=jnp.float32)
            spread = spread[:cells_xy] + spread[cells_xy:]
            first_row = reach * rows_y
            for q in range(2):
                middle = sources[q][first_row : first_row + cells_xy]
                along = jnp.dot(
                    jnp.concatenate([middle, middle], axis=1), line_mat[...], preferred_element_type=jnp.float32
                )
                total = spread[:, q * rows_z : (q + 1) * rows_z] + along + energy[...] * middle.astype(jnp.float32)
                if s == 0:
                    value = total * (sigma_one / width_e)
                else:
                    earlier = ext[s - 1][o + q, pl.ds(reach, planes)].reshape(cells_xy, rows_z).astype(jnp.float32)
                    if s == 1:
                        value = total * (2.0 * sigma_two / width_e) - (sigma_one * sigma_two) * earlier
                    else:
                        value = total * (2.0 * sigma_three / width_e) - (sigma_two * sigma_three) * earlier
                if s < 2:
                    ext[s + 1][o + q, pl.ds(reach, planes)] = value.astype(jnp.bfloat16).reshape(planes, rows_y, rows_z)
                else:
                    full[lax.rem(o, PACK) + q] = value
            return carry

        lax.fori_loop(0, GROUP // 2, pair, 0)

    def turn(h):
        def block(r, carry):
            at = pl.multiple_of(r * 8, 8)
            piece = full[:, pl.ds(at, 8), :]
            turned[h, pl.ds(at, 8)] = jnp.swapaxes(piece, 0, 1).astype(jnp.bfloat16)
            return carry

        lax.fori_loop(0, cells_xy // 8, block, 0)

    def share(h, k):
        target = lax.rem(band + k, nb)
        return remote(turned.at[h, pl.ds(target * part, part)], cols.at[band * packs + h],
                      share_s.at[h, k], share_r.at[h, k], (target, domain))

    scale_group(0)
    constants[0].wait()
    energy[...] = pot[...].reshape(cells_xy, rows_z) + (3.0 * stencil_coef[0] * kinetic - centre)
    pl.semaphore_wait(
        barrier, nb - 1 + places + levels - 1 + has_low.astype(jnp.int32) + has_high.astype(jnp.int32)
    )
    send_edges(0, 0)
    for g in range(1, LAG + 1):
        scale_group(g)
        send_edges(0, g)

    @pl.when(jnp.logical_not(has_low))
    def _():
        for s in range(STEPS):
            ext[s][:, :reach] = jnp.zeros((orbitals, reach, rows_y, rows_z), jnp.bfloat16)

    @pl.when(jnp.logical_not(has_high))
    def _():
        for s in range(STEPS):
            ext[s][:, planes + reach :] = jnp.zeros((orbitals, reach, rows_y, rows_z), jnp.bfloat16)

    for copy in constants[1:]:
        copy.wait()

    for t in range(groups + (STEPS - 1) * LAG):
        for s in range(STEPS):
            g = t - s * LAG
            if not 0 <= g < groups:
                continue
            await_edges(s, g)
            apply(s, g)
            if s < STEPS - 1:
                send_edges(s + 1, g)
            if s == 0 and g + LAG + 1 < groups:
                scale_group(g + LAG + 1)
                send_edges(0, g + LAG + 1)
            if s == STEPS - 1 and (g + 1) * GROUP % PACK == 0:
                h = g * GROUP // PACK
                turn(h)
                for k in range(1, nb):
                    share(h, k).start()
                cols[band * packs + h] = turned[h, pl.ds(band * part, part)]

    for h in range(packs):
        for k in range(1, nb):
            share(h, k).wait()

    total_orbitals = nb * orbitals

    def column(r):
        return cols[:, r].reshape(total_orbitals, rows_z)

    def gram_step(i, total):
        both = jnp.concatenate([column(2 * i), column(2 * i + 1)], axis=1)
        return total + lax.dot_general(both, both, (((1,), (1,)), ((), ())), preferred_element_type=jnp.float32)

    gram[...] = lax.fori_loop(0, part // 2, gram_step, jnp.zeros(gram.shape, jnp.float32))

    half_rows = total_orbitals // 2
    piece = half_rows // places
    mine_at = pl.multiple_of(core * half_rows, 8)
    other_at = pl.multiple_of((1 - core) * half_rows, 8)
    swap = remote(gram.at[pl.ds(other_at, half_rows)], half, core_s, core_r, partner)
    swap.start()
    swap.wait()
    half[...] += gram[pl.ds(mine_at, half_rows), :]

    copies = []
    for k in range(1, places):
        p = lax.rem(place + k, places)
        copy = remote(half.at[pl.ds(pl.multiple_of(p * piece, 8), piece)], rows.at[place],
                      plane_s.at[k], plane_r.at[k], at_place(p))
        copy.start()
        copies.append(copy)
    rows[place] = half[pl.ds(pl.multiple_of(place * piece, 8), piece), :]
    for copy in copies:
        copy.wait()
    total = rows[0]
    for k in range(1, places):
        total = total + rows[k]
    mine[...] = total

    copies = []
    for k in range(1, levels):
        l = lax.rem(level + k, levels)
        copy = remote(mine, line.at[level], line_s.at[k], line_r.at[k], at_level(l))
        copy.start()
        copies.append(copy)
    line[level] = mine[...]
    for copy in copies:
        copy.wait()
    total = line[0]
    for k in range(1, levels):
        total = total + line[k]
    own = pl.ds(pl.multiple_of(mine_at + place * piece, 8), piece)
    work[own, :] = total

    copies = []
    for k in range(1, places):
        p = lax.rem(place + k, places)
        copy = remote(work.at[own], work.at[own], back_s.at[k], back_r.at[k], at_place(p))
        copy.start()
        copies.append(copy)
    for copy in copies:
        copy.wait()
    span = pl.ds(mine_at, half_rows)
    final = remote(work.at[span], work.at[span], last_s, last_r, partner)
    final.start()
    final.wait()

    factor_inverse(cells, work, rot)

    rows_each = part // CHUNKS

    def home(c, k):
        target = lax.rem(band + k, nb)
        return remote(mixed.at[target, pl.ds(c * rows_each, rows_each)],
                      out_ref.at[pl.ds(band * part + c * rows_each, rows_each)],
                      home_s.at[c, k], home_r.at[c, k], (target, domain))

    for c in range(CHUNKS):
        def mix(i, carry):
            r = c * rows_each + 2 * i
            both = jnp.concatenate([column(r), column(r + 1)], axis=1)
            value = jnp.dot(rot[...], both, preferred_element_type=jnp.float32).astype(jnp.bfloat16)
            mixed[:, r] = value[:, :rows_z].reshape(nb, orbitals, rows_z)
            mixed[:, r + 1] = value[:, rows_z:].reshape(nb, orbitals, rows_z)
            return carry

        lax.fori_loop(0, rows_each // 2, mix, 0)
        for k in range(1, nb):
            home(c, k).start()

    out_ref[pl.ds(band * part, part)] = mixed[band]
    for c in range(CHUNKS):
        for k in range(1, nb):
            home(c, k).wait()
    for s in range(STEPS):
        for g in range(groups):
            @pl.when(has_high)
            def _():
                upward(s, g).wait_send()

            @pl.when(has_low)
            def _():
                downward(s, g).wait_send()


def factor_inverse(cells, work, out_ref):
    size = work.shape[0]
    panel = PANEL
    work[...] = work[...] * (1.0 / cells)
    lane = lax.broadcasted_iota(jnp.int32, (panel, size), 1)
    row = lax.broadcasted_iota(jnp.int32, (panel, size), 0)
    sub = lax.broadcasted_iota(jnp.int32, (panel, 128), 0)
    wide = lax.broadcasted_iota(jnp.int32, (size, size), 1)

    def step(k, carry):
        start = pl.multiple_of(k * panel, panel)
        tile = pl.multiple_of((start // 128) * 128, 128)
        here = pl.ds(start, panel)
        corner = pltpu.roll(work[here, pl.ds(tile, 128)], 128 - (start - tile), 1)
        rows = work[here, :]
        inside = (lane >= start) & (lane < start + panel)
        rows = jnp.where(inside, jnp.where(lane - start == row, 1.0, 0.0), rows)
        columns = [jnp.broadcast_to(corner[:, j : j + 1], (panel, 128)) for j in range(panel)]
        pivots = jnp.ones((panel, 128), jnp.float32)
        for j in range(panel):
            spread = [jnp.broadcast_to(columns[j][l : l + 1, :], (panel, 128)) for l in range(j, panel)]
            pivot = spread[0]
            pivots = jnp.where(sub == j, pivot, pivots)
            if j < panel - 1:
                factor = jnp.where(sub > j, columns[j] * (1.0 / pivot), 0.0)
                for l in range(j + 1, panel):
                    columns[l] = columns[l] - factor * spread[l - j]
                wide_factor = jnp.concatenate([factor] * (size // 128), axis=1)
                rows = rows - wide_factor * jnp.broadcast_to(rows[j : j + 1, :], (panel, size))
        scale = lax.rsqrt(pivots)
        rows = rows * jnp.concatenate([scale] * (size // 128), axis=1)
        below = jnp.where(lane >= start + panel, rows, 0.0)
        change = lax.dot_general(
            below, rows, (((0,), (0,)), ((), ())),
            precision=lax.Precision.HIGHEST, preferred_element_type=jnp.float32,
        )
        keep = (wide >= start) & (wide < start + panel)
        work[...] = jnp.where(keep, 0.0, work[...]) - change
        work[here, :] = rows
        return carry

    lax.fori_loop(0, size // panel, step, 0)
    down = lax.broadcasted_iota(jnp.int32, (size, size), 0)
    out_ref[...] = jnp.where(wide <= down, work[...], 0.0).astype(out_ref.dtype)


def fused_step(orbital_block, block_scale, potential, nx, ny, nzl, nzh):
    orbitals, planes, rows_y, rows_z = orbital_block.shape
    reach = len(stencil_coef) - 1
    plane_part, line_part = stencil_matrices(planes, rows_y, rows_z)
    cells_xy = planes * rows_y
    groups, packs = orbitals // GROUP, orbitals // PACK
    nb, nd = ny * nzh, nzl * nx * 2
    places, levels = nx * ny, nzl * nzh
    part, size = cells_xy // nb, nb * orbitals
    piece = size // 2 // places
    dma = pltpu.SemaphoreType.DMA
    f32, bf16 = jnp.float32, jnp.bfloat16
    hbm = pl.BlockSpec(memory_space=pl.ANY)
    wide = pltpu.VMEM((orbitals, planes + 2 * reach, rows_y, rows_z), bf16)
    edge = dma((STEPS, groups))
    return pl.pallas_call(
        functools.partial(step_kernel, nx, ny, nzl, nzh, float(cells_xy * rows_z * nd)),
        out_shape=jax.ShapeDtypeStruct((cells_xy, orbitals, rows_z), bf16),
        in_specs=[hbm, pl.BlockSpec(memory_space=pltpu.SMEM), hbm, hbm, hbm],
        out_specs=pl.BlockSpec(memory_space=pltpu.VMEM),
        scratch_shapes=[
            pltpu.VMEM(orbital_block.shape, bf16),
            pltpu.VMEM(potential.shape, f32),
            pltpu.VMEM(plane_part.shape, bf16),
            pltpu.VMEM(line_part.shape, bf16),
            wide, wide, wide,
            pltpu.VMEM((PACK, cells_xy, rows_z), f32),
            pltpu.VMEM((packs, cells_xy, PACK, rows_z), bf16),
            pltpu.VMEM((nb * packs, part, PACK, rows_z), bf16),
            pltpu.VMEM((cells_xy, rows_z), f32),
            pltpu.VMEM((size, size), f32),
            pltpu.VMEM((size // 2, size), f32),
            pltpu.VMEM((places, piece, size), f32),
            pltpu.VMEM((levels, piece, size), f32),
            pltpu.VMEM((piece, size), f32),
            pltpu.VMEM((size, size), f32),
            pltpu.VMEM((size, size), bf16),
            pltpu.VMEM((nb, part, orbitals, rows_z), bf16),
            dma((groups,)), dma((3,)), edge, edge, edge, edge, dma((packs, nb)), dma((packs, nb)),
            dma, dma, dma((places,)), dma((places,)), dma((levels,)), dma((levels,)),
            dma((places,)), dma((places,)), dma, dma, dma((CHUNKS, nb)), dma((CHUNKS, nb)),
        ],
        compiler_params=pltpu.CompilerParams(collective_id=1, has_side_effects=True, vmem_limit_bytes=60 << 20),
        name="filter_and_rotate",
    )(orbital_block, block_scale, potential, jnp.asarray(plane_part), jnp.asarray(line_part))


def solution(mesh):
    nzh, nzl, nx = 2, 4, 4
    ny = mesh.shape["band"] // nzh

    def body(orbital_block, block_scale, potential):
        back = fused_step(orbital_block, block_scale, potential, nx, ny, nzl, nzh)
        return back.transpose(1, 0, 2).reshape(orbital_block.shape)

    in_specs = (P("band", "domain", None, None), P("band", "domain"), P("domain", None, None))
    out_specs = P("band", "domain", None, None)
    return jax.shard_map(body, mesh=mesh, in_specs=in_specs, out_specs=out_specs, check_vma=False)
```

```python
import functools

import jax
import jax.numpy as jnp
import ml_dtypes
import numpy as np
from jax import lax
from jax.experimental import pallas as pl
from jax.experimental.pallas import tpu as pltpu
from jax.sharding import PartitionSpec as P

MESH = pl.DeviceIdType.MESH

grid_step = 0.5
stencil_coef = (
    -5369.0 / 1800.0,
    12.0 / 7.0,
    -15.0 / 56.0,
    10.0 / 189.0,
    -1.0 / 112.0,
    2.0 / 1925.0,
    -1.0 / 16632.0,
)
lower_end = -4.0
cut_energy = 6.0
upper_end = 43.0


def filter_terms():
    width_e = (upper_end - cut_energy) / 2.0
    centre = (upper_end + cut_energy) / 2.0
    sigma_one = width_e / (lower_end - centre)
    gamma_term = 2.0 / sigma_one
    sigma_two = 1.0 / (gamma_term - sigma_one)
    sigma_three = 1.0 / (gamma_term - sigma_two)
    return (width_e, centre, sigma_one, sigma_two, sigma_three)


def remote(src, dst, send_sem, recv_sem, device):
    return pltpu.make_async_remote_copy(
        src_ref=src, dst_ref=dst, send_sem=send_sem, recv_sem=recv_sem,
        device_id=device, device_id_type=MESH,
    )


def stencil_matrices(planes, rows_y, rows_z):
    reach = len(stencil_coef) - 1
    plane_part = np.zeros((planes, rows_y, planes + 2 * reach, rows_y), np.float64)
    line_part = np.zeros((2, rows_z, 2, rows_z), np.float64)
    for m in range(1, reach + 1):
        weight = stencil_coef[m] / stencil_coef[1]
        for sign in (-m, m):
            for x in range(planes):
                for y in range(rows_y):
                    plane_part[x, y, x + reach + sign, y] += weight
                    if 0 <= y + sign < rows_y:
                        plane_part[x, y, x + reach, y + sign] += weight
            for z in range(rows_z):
                if 0 <= z + sign < rows_z:
                    for q in range(2):
                        line_part[q, z + sign, q, z] += weight
    plane_part = plane_part.reshape(planes * rows_y, (planes + 2 * reach) * rows_y)
    line_part = line_part.reshape(2 * rows_z, 2 * rows_z)
    return plane_part.astype(ml_dtypes.bfloat16), line_part.astype(ml_dtypes.bfloat16)


GROUP = 4
PACK = 8
LAG = 2
STEPS = 3
CHUNKS = 8
UNROLL = True
AHEAD = 4
EARLY = 8
PANEL = 32


def step_kernel(
    nx, ny, nzl, nzh, cells,
    orb_hbm, scale_hbm, pot_hbm, plane_hbm, line_hbm, out_ref,
    orb, scale, spread_scale, pot, plane_mat, line_mat, ext0, ext1, ext2, full, turned, cols, energy,
    gram, half, rows, line, mine, work, rot, rot_own, mixed,
    load_s, const_s, up_s, up_r, down_s, down_r, share_s, share_r,
    core_s, core_r, plane_s, plane_r, line_s, line_r, back_s, back_r, last_s, last_r, home_s, home_r, ahead_s, ahead_r,
):
    nb, nd = ny * nzh, nzl * nx * 2
    band = lax.axis_index("band")
    domain = lax.axis_index("domain")
    orbitals, planes, rows_y, rows_z = orb.shape
    reach = len(stencil_coef) - 1
    cells_xy = planes * rows_y
    part = cells_xy // nb
    groups = orbitals // GROUP
    packs = orbitals // PACK
    ext = (ext0, ext1, ext2)
    has_low, has_high = domain > 0, domain < nd - 1
    width_e, centre, sigma_one, sigma_two, sigma_three = filter_terms()
    kinetic = -0.5 / (grid_step * grid_step)

    y, z_hi = band // nzh, lax.rem(band, nzh)
    core = lax.rem(domain, 2)
    x = lax.rem(domain // 2, nx)
    z_lo = domain // (2 * nx)
    place = y * nx + x
    places = nx * ny
    level = z_hi * nzl + z_lo
    levels = nzl * nzh
    partner = (band, domain + 1 - 2 * core)

    def at_place(p):
        return ((p // nx) * nzh + z_hi, (z_lo * nx + lax.rem(p, nx)) * 2 + core)

    def at_level(l):
        return (y * nzh + l // nzl, (lax.rem(l, nzl) * nx + x) * 2 + core)

    def load(g):
        some = pl.ds(g * GROUP, GROUP)
        return pltpu.make_async_copy(orb_hbm.at[some], orb.at[some], load_s.at[g])

    constants = [
        pltpu.make_async_copy(source, target, const_s.at[i])
        for i, (source, target) in enumerate(((scale_hbm, scale), (pot_hbm, pot), (plane_hbm, plane_mat), (line_hbm, line_mat)))
    ]
    constants[0].start()
    load(0).start()
    for copy in constants[1:]:
        copy.start()
    for g in range(1, groups):
        load(g).start()

    barrier = pltpu.get_barrier_semaphore()

    def greet(device):
        pl.semaphore_signal(barrier, inc=1, device_id=device, device_id_type=MESH)

    @pl.when(has_low)
    def _():
        greet((band, domain - 1))

    @pl.when(has_high)
    def _():
        greet((band, domain + 1))

    for k in range(1, nb):
        greet((lax.rem(band + k, nb), domain))
    greet(partner)
    for k in range(1, places):
        greet(at_place(lax.rem(place + k, places)))
    for k in range(1, levels):
        greet(at_level(lax.rem(level + k, levels)))

    def scale_group(g):
        load(g).wait()

        def one(i, carry):
            o = g * GROUP + i
            for p in range(planes):
                ext0[o, reach + p] = (orb[o, p].astype(jnp.float32) * spread_scale[p, pl.ds(o, 1), :]).astype(jnp.bfloat16)
            return carry

        lax.fori_loop(0, GROUP, one, 0)

    def upward(s, g):
        some = pl.ds(g * GROUP, GROUP)
        return remote(ext[s].at[some, pl.ds(planes, reach)], ext[s].at[some, pl.ds(0, reach)],
                      up_s.at[s, g], up_r.at[s, g], (band, domain + 1))

    def downward(s, g):
        some = pl.ds(g * GROUP, GROUP)
        return remote(ext[s].at[some, pl.ds(reach, reach)], ext[s].at[some, pl.ds(planes + reach, reach)],
                      down_s.at[s, g], down_r.at[s, g], (band, domain - 1))

    def send_edges(s, g):
        @pl.when(has_high)
        def _():
            upward(s, g).start()

        @pl.when(has_low)
        def _():
            downward(s, g).start()

    def await_edges(s, g):
        @pl.when(has_low)
        def _():
            upward(s, g).wait_recv()

        @pl.when(has_high)
        def _():
            downward(s, g).wait_recv()

    outer = (sigma_one / width_e, 2.0 * sigma_two / width_e, 2.0 * sigma_three / width_e)
    inner = (None, sigma_one * sigma_two, sigma_two * sigma_three)

    def apply(s, g):
        def pair(i, carry):
            o = g * GROUP + 2 * i
            sources = [ext[s][o + q].reshape((planes + 2 * reach) * rows_y, rows_z) for q in range(2)]
            both = jnp.concatenate(sources, axis=1)
            middle = both[reach * rows_y : reach * rows_y + cells_xy]
            spread = jnp.dot(plane_mat[...], both, preferred_element_type=jnp.float32)
            spread = spread + jnp.dot(middle, line_mat[...], preferred_element_type=jnp.float32)
            for q in range(2):
                lanes = slice(q * rows_z, (q + 1) * rows_z)
                value = spread[:, lanes] * (outer[s] * kinetic * stencil_coef[1])
                value = value + energy[s] * middle[:, lanes].astype(jnp.float32)
                if s > 0:
                    earlier = ext[s - 1][o + q, pl.ds(reach, planes)].reshape(cells_xy, rows_z)
                    value = value - inner[s] * earlier.astype(jnp.float32)
                if s < STEPS - 1:
                    ext[s + 1][o + q, pl.ds(reach, planes)] = value.astype(jnp.bfloat16).reshape(planes, rows_y, rows_z)
                else:
                    full[lax.rem(o, PACK) + q] = value
            return carry

        lax.fori_loop(0, GROUP // 2, pair, 0, unroll=UNROLL)

    def turn(h):
        def block(r, carry):
            at = pl.multiple_of(r * 8, 8)
            piece = full[:, pl.ds(at, 8), :]
            turned[h, pl.ds(at, 8)] = jnp.swapaxes(piece, 0, 1).astype(jnp.bfloat16)
            return carry

        lax.fori_loop(0, cells_xy // 8, block, 0)

    span_rows = part * nzh
    my_rows = pl.ds(pl.multiple_of(z_hi * part, 8), part)

    def same_share(h, k):
        target = lax.rem(y + k, ny)
        return remote(turned.at[h, pl.ds(target * span_rows, span_rows)], cols.at[band * packs + h],
                      share_s.at[h, k], share_r.at[h, k], (target * nzh + z_hi, domain))

    def cross_share(h, k):
        target = lax.rem(y + k, ny)
        there = 1 - z_hi
        rows_there = pl.ds(pl.multiple_of(there * part, 8), part)
        return remote(turned.at[h, pl.ds(pl.multiple_of((target * nzh + there) * part, 8), part)],
                      cols.at[band * packs + h, rows_there],
                      share_s.at[h, ny + k], share_r.at[h, ny + k], (target * nzh + there, domain))

    def shares(h):
        return [cross_share(h, k) for k in range(ny)] + [same_share(h, k) for k in range(1, ny)]

    def ahead(i):
        pack = (2 * (i // packs) + z_hi) * packs + i % packs
        return remote(cols.at[pack, my_rows], cols.at[pack, my_rows], ahead_s.at[i], ahead_r.at[i],
                      (y * nzh + 1 - z_hi, domain))

    constants[0].wait()
    upright = scale[...].T
    for p in range(planes):
        spread_scale[p] = jnp.broadcast_to(upright[:, p : p + 1], (orbitals, rows_z))
    for g in range(EARLY):
        scale_group(g)
    constants[1].wait()
    shifted = pot[...].reshape(cells_xy, rows_z) + (3.0 * stencil_coef[0] * kinetic - centre)
    for s in range(STEPS):
        energy[s] = shifted * outer[s]
    pl.semaphore_wait(
        barrier, nb - 1 + places + levels - 1 + has_low.astype(jnp.int32) + has_high.astype(jnp.int32)
    )
    for g in range(LAG + 1):
        send_edges(0, g)

    @pl.when(jnp.logical_not(has_low))
    def _():
        for s in range(STEPS):
            ext[s][:, :reach] = jnp.zeros((orbitals, reach, rows_y, rows_z), jnp.bfloat16)

    @pl.when(jnp.logical_not(has_high))
    def _():
        for s in range(STEPS):
            ext[s][:, planes + reach :] = jnp.zeros((orbitals, reach, rows_y, rows_z), jnp.bfloat16)

    for copy in constants[2:]:
        copy.wait()

    for t in range(groups + (STEPS - 1) * LAG):
        for s in range(STEPS):
            g = t - s * LAG
            if not 0 <= g < groups:
                continue
            await_edges(s, g)
            apply(s, g)
            if s < STEPS - 1:
                send_edges(s + 1, g)
            if s == 0 and g + LAG + 1 < groups:
                if g + LAG + 1 >= EARLY:
                    scale_group(g + LAG + 1)
                send_edges(0, g + LAG + 1)
            if s == STEPS - 1 and (g + 1) * GROUP % PACK == 0:
                h = g * GROUP // PACK
                turn(h)
                for copy in shares(h):
                    copy.start()
                cols[band * packs + h] = turned[h, pl.ds(y * span_rows, span_rows)]

    for h in range(packs):
        for copy in shares(h):
            copy.wait()
    for i in range(AHEAD):
        ahead(i).start()

    total_orbitals = nb * orbitals

    def column(r):
        return cols[:, r].reshape(total_orbitals, rows_z)

    def gram_step(i, total):
        r = z_hi * part + 2 * i
        both = jnp.concatenate([column(r), column(r + 1)], axis=1)
        return total + lax.dot_general(both, both, (((1,), (1,)), ((), ())), preferred_element_type=jnp.float32)

    gram[...] = lax.fori_loop(0, part // 2, gram_step, jnp.zeros(gram.shape, jnp.float32))

    half_rows = total_orbitals // 2
    piece = half_rows // places
    mine_at = pl.multiple_of(core * half_rows, 8)
    other_at = pl.multiple_of((1 - core) * half_rows, 8)
    swap = remote(gram.at[pl.ds(other_at, half_rows)], half, core_s, core_r, partner)
    swap.start()
    swap.wait()
    half[...] += gram[pl.ds(mine_at, half_rows), :]

    copies = []
    for k in range(1, places):
        p = lax.rem(place + k, places)
        copy = remote(half.at[pl.ds(pl.multiple_of(p * piece, 8), piece)], rows.at[place],
                      plane_s.at[k], plane_r.at[k], at_place(p))
        copy.start()
        copies.append(copy)
    rows[place] = half[pl.ds(pl.multiple_of(place * piece, 8), piece), :]
    for copy in copies:
        copy.wait()
    total = rows[0]
    for k in range(1, places):
        total = total + rows[k]
    mine[...] = total

    copies = []
    for k in range(1, levels):
        l = lax.rem(level + k, levels)
        copy = remote(mine, line.at[level], line_s.at[k], line_r.at[k], at_level(l))
        copy.start()
        copies.append(copy)
    line[level] = mine[...]
    for copy in copies:
        copy.wait()
    for i in range(AHEAD, ny * packs):
        ahead(i).start()
    total = line[0]
    for k in range(1, levels):
        total = total + line[k]
    own = pl.ds(pl.multiple_of(mine_at + place * piece, 8), piece)
    work[own, :] = total

    copies = []
    for k in range(1, places):
        p = lax.rem(place + k, places)
        copy = remote(work.at[own], work.at[own], back_s.at[k], back_r.at[k], at_place(p))
        copy.start()
        copies.append(copy)
    for copy in copies:
        copy.wait()
    span = pl.ds(mine_at, half_rows)
    final = remote(work.at[span], work.at[span], last_s, last_r, partner)
    final.start()
    final.wait()

    factor_inverse(cells, work, rot)

    for k in range(ny):
        rot_own[pl.ds(k * orbitals, orbitals), :] = rot[pl.ds(pl.multiple_of((k * nzh + z_hi) * orbitals, orbitals), orbitals), :]
    rows_each = span_rows // CHUNKS

    def chunk_row(c):
        return pl.multiple_of(lax.rem(z_hi * part + c * rows_each, span_rows), 2)

    def home(c, k):
        target = lax.rem(y + k, ny)
        first = chunk_row(c)
        return remote(mixed.at[target, pl.ds(first, rows_each)],
                      out_ref.at[pl.ds(y * span_rows + first, rows_each)],
                      home_s.at[c, k], home_r.at[c, k], (target * nzh + z_hi, domain))

    for c in range(CHUNKS):
        if c == CHUNKS // 2:
            for i in range(ny * packs):
                ahead(i).wait()

        def mix(i, carry):
            r = chunk_row(c) + 2 * i
            both = jnp.concatenate([column(r), column(r + 1)], axis=1)
            value = jnp.dot(rot_own[...], both, preferred_element_type=jnp.float32).astype(jnp.bfloat16)
            mixed[:, r] = value[:, :rows_z].reshape(ny, orbitals, rows_z)
            mixed[:, r + 1] = value[:, rows_z:].reshape(ny, orbitals, rows_z)
            return carry

        lax.fori_loop(0, rows_each // 2, mix, 0)
        for k in range(1, ny):
            home(c, k).start()

    out_ref[pl.ds(y * span_rows, span_rows)] = mixed[y]
    for c in range(CHUNKS):
        for k in range(1, ny):
            home(c, k).wait()
    for s in range(STEPS):
        for g in range(groups):
            @pl.when(has_high)
            def _():
                upward(s, g).wait_send()

            @pl.when(has_low)
            def _():
                downward(s, g).wait_send()


def factor_inverse(cells, work, out_ref):
    size = work.shape[0]
    panel = PANEL
    work[...] = work[...] * (1.0 / cells)
    lane = lax.broadcasted_iota(jnp.int32, (panel, size), 1)
    row = lax.broadcasted_iota(jnp.int32, (panel, size), 0)
    sub = lax.broadcasted_iota(jnp.int32, (panel, 128), 0)
    wide = lax.broadcasted_iota(jnp.int32, (size, size), 1)

    def step(k, carry):
        start = pl.multiple_of(k * panel, panel)
        tile = pl.multiple_of((start // 128) * 128, 128)
        here = pl.ds(start, panel)
        corner = pltpu.roll(work[here, pl.ds(tile, 128)], 128 - (start - tile), 1)
        rows = work[here, :]
        inside = (lane >= start) & (lane < start + panel)
        rows = jnp.where(inside, jnp.where(lane - start == row, 1.0, 0.0), rows)
        columns = [jnp.broadcast_to(corner[:, j : j + 1], (panel, 128)) for j in range(panel)]
        pivots = jnp.ones((panel, 128), jnp.float32)
        for j in range(panel):
            spread = [jnp.broadcast_to(columns[j][l : l + 1, :], (panel, 128)) for l in range(j, panel)]
            pivot = spread[0]
            pivots = jnp.where(sub == j, pivot, pivots)
            if j < panel - 1:
                factor = jnp.where(sub > j, columns[j] * (1.0 / pivot), 0.0)
                for l in range(j + 1, panel):
                    columns[l] = columns[l] - factor * spread[l - j]
                wide_factor = jnp.concatenate([factor] * (size // 128), axis=1)
                rows = rows - wide_factor * jnp.broadcast_to(rows[j : j + 1, :], (panel, size))
        scale = lax.rsqrt(pivots)
        rows = rows * jnp.concatenate([scale] * (size // 128), axis=1)
        below = jnp.where(lane >= start + panel, rows, 0.0)
        change = lax.dot_general(
            below, rows, (((0,), (0,)), ((), ())),
            precision=lax.Precision.HIGHEST, preferred_element_type=jnp.float32,
        )
        keep = (wide >= start) & (wide < start + panel)
        work[...] = jnp.where(keep, 0.0, work[...]) - change
        work[here, :] = rows
        return carry

    lax.fori_loop(0, size // panel, step, 0)
    down = lax.broadcasted_iota(jnp.int32, (size, size), 0)
    out_ref[...] = jnp.where(wide <= down, work[...], 0.0).astype(out_ref.dtype)


def fused_step(orbital_block, block_scale, potential, nx, ny, nzl, nzh):
    orbitals, planes, rows_y, rows_z = orbital_block.shape
    reach = len(stencil_coef) - 1
    plane_part, line_part = stencil_matrices(planes, rows_y, rows_z)
    cells_xy = planes * rows_y
    groups, packs = orbitals // GROUP, orbitals // PACK
    nb, nd = ny * nzh, nzl * nx * 2
    places, levels = nx * ny, nzl * nzh
    part, size = cells_xy // nb, nb * orbitals
    piece = size // 2 // places
    dma = pltpu.SemaphoreType.DMA
    f32, bf16 = jnp.float32, jnp.bfloat16
    hbm = pl.BlockSpec(memory_space=pltpu.HBM)
    wide = pltpu.VMEM((orbitals, planes + 2 * reach, rows_y, rows_z), bf16)
    edge = dma((STEPS, groups))
    return pl.pallas_call(
        functools.partial(step_kernel, nx, ny, nzl, nzh, float(cells_xy * rows_z * nd)),
        out_shape=jax.ShapeDtypeStruct((cells_xy, orbitals, rows_z), bf16),
        in_specs=[hbm] * 5,
        out_specs=pl.BlockSpec(memory_space=pltpu.VMEM),
        scratch_shapes=[
            pltpu.VMEM(orbital_block.shape, bf16),
            pltpu.VMEM(block_scale.shape[::-1], f32),
            pltpu.VMEM((planes, orbitals, rows_z), f32),
            pltpu.VMEM(potential.shape, f32),
            pltpu.VMEM(plane_part.shape, bf16),
            pltpu.VMEM(line_part.shape, bf16),
            wide, wide, wide,
            pltpu.VMEM((PACK, cells_xy, rows_z), f32),
            pltpu.VMEM((packs, cells_xy, PACK, rows_z), bf16),
            pltpu.VMEM((nb * packs, part * nzh, PACK, rows_z), bf16),
            pltpu.VMEM((STEPS, cells_xy, rows_z), f32),
            pltpu.VMEM((size, size), f32),
            pltpu.VMEM((size // 2, size), f32),
            pltpu.VMEM((places, piece, size), f32),
            pltpu.VMEM((levels, piece, size), f32),
            pltpu.VMEM((piece, size), f32),
            pltpu.VMEM((size, size), f32),
            pltpu.VMEM((size, size), bf16),
            pltpu.VMEM((ny * orbitals, size), bf16),
            pltpu.VMEM((ny, part * nzh, orbitals, rows_z), bf16),
            dma((groups,)), dma((4,)), edge, edge, edge, edge, dma((packs, nb)), dma((packs, nb)),
            dma, dma, dma((places,)), dma((places,)), dma((levels,)), dma((levels,)),
            dma((places,)), dma((places,)), dma, dma, dma((CHUNKS, ny)), dma((CHUNKS, ny)),
            dma((ny * packs,)), dma((ny * packs,)),
        ],
        compiler_params=pltpu.CompilerParams(collective_id=1, has_side_effects=True, vmem_limit_bytes=56 << 20),
        name="filter_and_rotate",
    )(orbital_block, block_scale.T, potential, jnp.asarray(plane_part), jnp.asarray(line_part))


def solution(mesh):
    nzh, nzl, nx = 2, 4, 4
    ny = mesh.shape["band"] // nzh

    def body(orbital_block, block_scale, potential):
        back = fused_step(orbital_block, block_scale, potential, nx, ny, nzl, nzh)
        return back.transpose(1, 0, 2).reshape(orbital_block.shape)

    in_specs = (P("band", "domain", None, None), P("band", "domain"), P("domain", None, None))
    out_specs = P("band", "domain", None, None)
    return jax.shard_map(body, mesh=mesh, in_specs=in_specs, out_specs=out_specs, check_vma=False)
```

```python
import functools

import jax
import jax.numpy as jnp
import ml_dtypes
import numpy as np
from jax import lax
from jax.experimental import pallas as pl
from jax.experimental.pallas import tpu as pltpu
from jax.sharding import PartitionSpec as P

MESH = pl.DeviceIdType.MESH

grid_step = 0.5
stencil_coef = (
    -5369.0 / 1800.0,
    12.0 / 7.0,
    -15.0 / 56.0,
    10.0 / 189.0,
    -1.0 / 112.0,
    2.0 / 1925.0,
    -1.0 / 16632.0,
)
lower_end = -4.0
cut_energy = 6.0
upper_end = 43.0


def filter_terms():
    width_e = (upper_end - cut_energy) / 2.0
    centre = (upper_end + cut_energy) / 2.0
    sigma_one = width_e / (lower_end - centre)
    gamma_term = 2.0 / sigma_one
    sigma_two = 1.0 / (gamma_term - sigma_one)
    sigma_three = 1.0 / (gamma_term - sigma_two)
    return (width_e, centre, sigma_one, sigma_two, sigma_three)


def remote(src, dst, send_sem, recv_sem, device):
    return pltpu.make_async_remote_copy(
        src_ref=src, dst_ref=dst, send_sem=send_sem, recv_sem=recv_sem,
        device_id=device, device_id_type=MESH,
    )


def stencil_matrices(planes, rows_y, rows_z):
    reach = len(stencil_coef) - 1
    plane_part = np.zeros((planes, rows_y, planes + 2 * reach, rows_y), np.float64)
    line_part = np.zeros((2, rows_z, 2, rows_z), np.float64)
    for m in range(1, reach + 1):
        weight = stencil_coef[m] / stencil_coef[1]
        for sign in (-m, m):
            for x in range(planes):
                for y in range(rows_y):
                    plane_part[x, y, x + reach + sign, y] += weight
                    if 0 <= y + sign < rows_y:
                        plane_part[x, y, x + reach, y + sign] += weight
            for z in range(rows_z):
                if 0 <= z + sign < rows_z:
                    for q in range(2):
                        line_part[q, z + sign, q, z] += weight
    plane_part = plane_part.reshape(planes * rows_y, (planes + 2 * reach) * rows_y)
    line_part = line_part.reshape(2 * rows_z, 2 * rows_z)
    return plane_part.astype(ml_dtypes.bfloat16), line_part.astype(ml_dtypes.bfloat16)


GROUP = 4
PACK = 8
LAG = 3
STEPS = 3
CHUNKS = 12
UNROLL = True
AHEAD = 1
EARLY = 8
PANEL = 32


def step_kernel(
    nx, ny, nzl, nzh, cells,
    orb_hbm, scale_hbm, pot_hbm, plane_hbm, line_hbm, out_ref,
    orb, scale, spread_scale, pot, plane_mat, line_mat, ext0, ext1, ext2, full, turned, cols, energy,
    gram, half, rows, line, mine, work, rot, rot_own, mixed,
    load_s, const_s, up_s, up_r, down_s, down_r, share_s, share_r,
    core_s, core_r, plane_s, plane_r, line_s, line_r, back_s, back_r, last_s, last_r, home_s, home_r, ahead_s, ahead_r,
):
    nb, nd = ny * nzh, nzl * nx * 2
    band = lax.axis_index("band")
    domain = lax.axis_index("domain")
    orbitals, planes, rows_y, rows_z = orb.shape
    reach = len(stencil_coef) - 1
    cells_xy = planes * rows_y
    part = cells_xy // nb
    groups = orbitals // GROUP
    packs = orbitals // PACK
    ext = (ext0, ext1, ext2)
    has_low, has_high = domain > 0, domain < nd - 1
    width_e, centre, sigma_one, sigma_two, sigma_three = filter_terms()
    kinetic = -0.5 / (grid_step * grid_step)

    y, z_hi = band // nzh, lax.rem(band, nzh)
    core = lax.rem(domain, 2)
    x = lax.rem(domain // 2, nx)
    z_lo = domain // (2 * nx)
    place = y * nx + x
    places = nx * ny
    level = z_hi * nzl + z_lo
    levels = nzl * nzh
    partner = (band, domain + 1 - 2 * core)

    def at_place(p):
        return ((p // nx) * nzh + z_hi, (z_lo * nx + lax.rem(p, nx)) * 2 + core)

    def at_level(l):
        return (y * nzh + l // nzl, (lax.rem(l, nzl) * nx + x) * 2 + core)

    def load(g):
        some = pl.ds(g * GROUP, GROUP)
        return pltpu.make_async_copy(orb_hbm.at[some], orb.at[some], load_s.at[g])

    constants = [
        pltpu.make_async_copy(source, target, const_s.at[i])
        for i, (source, target) in enumerate(((scale_hbm, scale), (pot_hbm, pot), (plane_hbm, plane_mat), (line_hbm, line_mat)))
    ]
    constants[0].start()
    load(0).start()
    for copy in constants[1:]:
        copy.start()
    for g in range(1, groups):
        load(g).start()

    barrier = pltpu.get_barrier_semaphore()

    def greet(device):
        pl.semaphore_signal(barrier, inc=1, device_id=device, device_id_type=MESH)

    @pl.when(has_low)
    def _():
        greet((band, domain - 1))

    @pl.when(has_high)
    def _():
        greet((band, domain + 1))

    for k in range(1, nb):
        greet((lax.rem(band + k, nb), domain))
    greet(partner)
    for k in range(1, places):
        greet(at_place(lax.rem(place + k, places)))
    for k in range(1, levels):
        greet(at_level(lax.rem(level + k, levels)))

    def scale_group(g):
        load(g).wait()

        def one(i, carry):
            o = g * GROUP + i
            for p in range(planes):
                ext0[o, reach + p] = (orb[o, p].astype(jnp.float32) * spread_scale[p, pl.ds(o, 1), :]).astype(jnp.bfloat16)
            return carry

        lax.fori_loop(0, GROUP, one, 0)

    def upward(s, g):
        some = pl.ds(g * GROUP, GROUP)
        return remote(ext[s].at[some, pl.ds(planes, reach)], ext[s].at[some, pl.ds(0, reach)],
                      up_s.at[s, g], up_r.at[s, g], (band, domain + 1))

    def downward(s, g):
        some = pl.ds(g * GROUP, GROUP)
        return remote(ext[s].at[some, pl.ds(reach, reach)], ext[s].at[some, pl.ds(planes + reach, reach)],
                      down_s.at[s, g], down_r.at[s, g], (band, domain - 1))

    def send_edges(s, g):
        @pl.when(has_high)
        def _():
            upward(s, g).start()

        @pl.when(has_low)
        def _():
            downward(s, g).start()

    def await_edges(s, g):
        @pl.when(has_low)
        def _():
            upward(s, g).wait_recv()

        @pl.when(has_high)
        def _():
            downward(s, g).wait_recv()

    outer = (sigma_one / width_e, 2.0 * sigma_two / width_e, 2.0 * sigma_three / width_e)
    inner = (None, sigma_one * sigma_two, sigma_two * sigma_three)

    def apply(s, g):
        def pair(i, carry):
            o = g * GROUP + 2 * i
            sources = [ext[s][o + q].reshape((planes + 2 * reach) * rows_y, rows_z) for q in range(2)]
            both = jnp.concatenate(sources, axis=1)
            middle = both[reach * rows_y : reach * rows_y + cells_xy]
            spread = jnp.dot(plane_mat[...], both, preferred_element_type=jnp.float32)
            spread = spread + jnp.dot(middle, line_mat[...], preferred_element_type=jnp.float32)
            for q in range(2):
                lanes = slice(q * rows_z, (q + 1) * rows_z)
                value = spread[:, lanes] * (outer[s] * kinetic * stencil_coef[1])
                value = value + energy[s] * middle[:, lanes].astype(jnp.float32)
                if s > 0:
                    earlier = ext[s - 1][o + q, pl.ds(reach, planes)].reshape(cells_xy, rows_z)
                    value = value - inner[s] * earlier.astype(jnp.float32)
                if s < STEPS - 1:
                    ext[s + 1][o + q, pl.ds(reach, planes)] = value.astype(jnp.bfloat16).reshape(planes, rows_y, rows_z)
                else:
                    full[lax.rem(o, PACK) + q] = value
            return carry

        lax.fori_loop(0, GROUP // 2, pair, 0, unroll=UNROLL)

    def turn(h):
        def block(r, carry):
            at = pl.multiple_of(r * 8, 8)
            piece = full[:, pl.ds(at, 8), :]
            turned[h, pl.ds(at, 8)] = jnp.swapaxes(piece, 0, 1).astype(jnp.bfloat16)
            return carry

        lax.fori_loop(0, cells_xy // 8, block, 0)

    span_rows = part * nzh
    my_rows = pl.ds(pl.multiple_of(z_hi * part, 8), part)

    def same_share(h, k):
        target = lax.rem(y + k, ny)
        return remote(turned.at[h, pl.ds(target * span_rows, span_rows)], cols.at[band * packs + h],
                      share_s.at[h, k], share_r.at[h, k], (target * nzh + z_hi, domain))

    def cross_share(h, k):
        target = lax.rem(y + k, ny)
        there = 1 - z_hi
        rows_there = pl.ds(pl.multiple_of(there * part, 8), part)
        return remote(turned.at[h, pl.ds(pl.multiple_of((target * nzh + there) * part, 8), part)],
                      cols.at[band * packs + h, rows_there],
                      share_s.at[h, ny + k], share_r.at[h, ny + k], (target * nzh + there, domain))

    def shares(h):
        return [cross_share(h, k) for k in range(ny)] + [same_share(h, k) for k in range(1, ny)]

    rows_each = span_rows // CHUNKS
    blocks = part // rows_each
    opposite = (y * nzh + 1 - z_hi, domain)

    def ahead(i, k):
        rows_i = pl.ds(pl.multiple_of(z_hi * part + i * rows_each, 2), rows_each)
        block = cols.at[pl.ds((k * nzh + z_hi) * packs, packs), rows_i]
        return remote(block, block, ahead_s.at[i, k], ahead_r.at[i, k], opposite)

    def ahead_start(i):
        for k in range(ny - 1):
            ahead(i, k).start()

        @pl.when(z_hi == 0)
        def _():
            ahead(i, ny - 1).start()

    def ahead_wait(i):
        for k in range(ny - 1):
            ahead(i, k).wait()

        @pl.when(z_hi == 0)
        def _():
            ahead(i, ny - 1).wait_send()

        @pl.when(z_hi == 1)
        def _():
            ahead(i, ny - 1).wait_recv()

    constants[0].wait()
    upright = scale[...].T
    for p in range(planes):
        spread_scale[p] = jnp.broadcast_to(upright[:, p : p + 1], (orbitals, rows_z))
    for g in range(EARLY):
        scale_group(g)
    constants[1].wait()
    shifted = pot[...].reshape(cells_xy, rows_z) + (3.0 * stencil_coef[0] * kinetic - centre)
    for s in range(STEPS):
        energy[s] = shifted * outer[s]
    pl.semaphore_wait(
        barrier, nb - 1 + places + levels - 1 + has_low.astype(jnp.int32) + has_high.astype(jnp.int32)
    )
    for g in range(LAG + 1):
        send_edges(0, g)

    @pl.when(jnp.logical_not(has_low))
    def _():
        for s in range(STEPS):
            ext[s][:, :reach] = jnp.zeros((orbitals, reach, rows_y, rows_z), jnp.bfloat16)

    @pl.when(jnp.logical_not(has_high))
    def _():
        for s in range(STEPS):
            ext[s][:, planes + reach :] = jnp.zeros((orbitals, reach, rows_y, rows_z), jnp.bfloat16)

    for copy in constants[2:]:
        copy.wait()

    for t in range(groups + (STEPS - 1) * LAG):
        for s in range(STEPS):
            g = t - s * LAG
            if not 0 <= g < groups:
                continue
            await_edges(s, g)
            apply(s, g)
            if s < STEPS - 1:
                send_edges(s + 1, g)
            if s == 0 and g + LAG + 1 < groups:
                if g + LAG + 1 >= EARLY:
                    scale_group(g + LAG + 1)
                send_edges(0, g + LAG + 1)
            if s == STEPS - 1 and (g + 1) * GROUP % PACK == 0:
                h = g * GROUP // PACK
                turn(h)
                for copy in shares(h):
                    copy.start()
                cols[band * packs + h] = turned[h, pl.ds(y * span_rows, span_rows)]

    for h in range(packs):
        for copy in shares(h):
            copy.wait()
    for i in range(AHEAD):
        ahead_start(i)

    @pl.when(z_hi == 0)
    def _():
        cols[pl.ds((nb - 1) * packs, packs), pl.ds(part, part)] = jnp.zeros((packs, part, PACK, rows_z), jnp.bfloat16)


    total_orbitals = nb * orbitals

    def column(r):
        return cols[:, r].reshape(total_orbitals, rows_z)

    def gram_step(i, total):
        r = z_hi * part + 2 * i
        both = jnp.concatenate([column(r), column(r + 1)], axis=1)
        return total + lax.dot_general(both, both, (((1,), (1,)), ((), ())), preferred_element_type=jnp.float32)

    gram[...] = lax.fori_loop(0, part // 2, gram_step, jnp.zeros(gram.shape, jnp.float32))

    half_rows = total_orbitals // 2
    piece = half_rows // places
    mine_at = pl.multiple_of(core * half_rows, 8)
    other_at = pl.multiple_of((1 - core) * half_rows, 8)
    swap = remote(gram.at[pl.ds(other_at, half_rows)], half, core_s, core_r, partner)
    swap.start()
    swap.wait()
    half[...] += gram[pl.ds(mine_at, half_rows), :]

    copies = []
    for k in range(1, places):
        p = lax.rem(place + k, places)
        copy = remote(half.at[pl.ds(pl.multiple_of(p * piece, 8), piece)], rows.at[place],
                      plane_s.at[k], plane_r.at[k], at_place(p))
        copy.start()
        copies.append(copy)
    rows[place] = half[pl.ds(pl.multiple_of(place * piece, 8), piece), :]
    for copy in copies:
        copy.wait()
    total = rows[0]
    for k in range(1, places):
        total = total + rows[k]
    mine[...] = total

    copies = []
    for k in range(1, levels):
        l = lax.rem(level + k, levels)
        copy = remote(mine, line.at[level], line_s.at[k], line_r.at[k], at_level(l))
        copy.start()
        copies.append(copy)
    line[level] = mine[...]
    for copy in copies:
        copy.wait()
    for i in range(AHEAD, blocks):
        ahead_start(i)
    total = line[0]
    for k in range(1, levels):
        total = total + line[k]
    own = pl.ds(pl.multiple_of(mine_at + place * piece, 8), piece)
    work[own, :] = total

    copies = []
    for k in range(1, places):
        p = lax.rem(place + k, places)
        copy = remote(work.at[own], work.at[own], back_s.at[k], back_r.at[k], at_place(p))
        copy.start()
        copies.append(copy)
    for copy in copies:
        copy.wait()
    span = pl.ds(mine_at, half_rows)
    final = remote(work.at[span], work.at[span], last_s, last_r, partner)
    final.start()
    final.wait()

    factor_inverse(cells, work, rot)

    for k in range(ny):
        rot_own[pl.ds(k * orbitals, orbitals), :] = rot[pl.ds(pl.multiple_of((k * nzh + z_hi) * orbitals, orbitals), orbitals), :]
    def chunk_row(c):
        return pl.multiple_of(lax.rem(z_hi * part + c * rows_each, span_rows), 2)

    def home(c, k):
        target = lax.rem(y + k, ny)
        first = chunk_row(c)
        return remote(mixed.at[target, pl.ds(first, rows_each)],
                      out_ref.at[pl.ds(y * span_rows + first, rows_each)],
                      home_s.at[c, k], home_r.at[c, k], (target * nzh + z_hi, domain))

    for c in range(CHUNKS):
        if c >= blocks:
            ahead_wait(c - blocks)

        def mix(i, carry):
            r = chunk_row(c) + 2 * i
            both = jnp.concatenate([column(r), column(r + 1)], axis=1)
            value = jnp.dot(rot_own[...], both, preferred_element_type=jnp.float32).astype(jnp.bfloat16)
            mixed[:, r] = value[:, :rows_z].reshape(ny, orbitals, rows_z)
            mixed[:, r + 1] = value[:, rows_z:].reshape(ny, orbitals, rows_z)
            return carry

        lax.fori_loop(0, rows_each // 2, mix, 0)
        for k in range(1, ny):
            home(c, k).start()

    out_ref[pl.ds(y * span_rows, span_rows)] = mixed[y]
    for c in range(CHUNKS):
        for k in range(1, ny):
            home(c, k).wait()
    for s in range(STEPS):
        for g in range(groups):
            @pl.when(has_high)
            def _():
                upward(s, g).wait_send()

            @pl.when(has_low)
            def _():
                downward(s, g).wait_send()


def factor_inverse(cells, work, out_ref):
    size = work.shape[0]
    panel = PANEL
    work[...] = work[...] * (1.0 / cells)
    lane = lax.broadcasted_iota(jnp.int32, (panel, size), 1)
    row = lax.broadcasted_iota(jnp.int32, (panel, size), 0)
    sub = lax.broadcasted_iota(jnp.int32, (panel, 128), 0)
    wide = lax.broadcasted_iota(jnp.int32, (size, size), 1)

    def step(k, carry):
        start = pl.multiple_of(k * panel, panel)
        tile = pl.multiple_of((start // 128) * 128, 128)
        here = pl.ds(start, panel)
        corner = pltpu.roll(work[here, pl.ds(tile, 128)], 128 - (start - tile), 1)
        rows = work[here, :]
        inside = (lane >= start) & (lane < start + panel)
        rows = jnp.where(inside, jnp.where(lane - start == row, 1.0, 0.0), rows)
        columns = [jnp.broadcast_to(corner[:, j : j + 1], (panel, 128)) for j in range(panel)]
        pivots = jnp.ones((panel, 128), jnp.float32)
        for j in range(panel):
            spread = [jnp.broadcast_to(columns[j][l : l + 1, :], (panel, 128)) for l in range(j, panel)]
            pivot = spread[0]
            pivots = jnp.where(sub == j, pivot, pivots)
            if j < panel - 1:
                factor = jnp.where(sub > j, columns[j] * (1.0 / pivot), 0.0)
                for l in range(j + 1, panel):
                    columns[l] = columns[l] - factor * spread[l - j]
                wide_factor = jnp.concatenate([factor] * (size // 128), axis=1)
                rows = rows - wide_factor * jnp.broadcast_to(rows[j : j + 1, :], (panel, size))
        scale = lax.rsqrt(pivots)
        rows = rows * jnp.concatenate([scale] * (size // 128), axis=1)
        below = jnp.where(lane >= start + panel, rows, 0.0)
        change = lax.dot_general(
            below, rows, (((0,), (0,)), ((), ())),
            precision=lax.Precision.HIGHEST, preferred_element_type=jnp.float32,
        )
        keep = (wide >= start) & (wide < start + panel)
        work[...] = jnp.where(keep, 0.0, work[...]) - change
        work[here, :] = rows
        return carry

    lax.fori_loop(0, size // panel, step, 0)
    down = lax.broadcasted_iota(jnp.int32, (size, size), 0)
    out_ref[...] = jnp.where(wide <= down, work[...], 0.0).astype(out_ref.dtype)


def fused_step(orbital_block, block_scale, potential, nx, ny, nzl, nzh):
    orbitals, planes, rows_y, rows_z = orbital_block.shape
    reach = len(stencil_coef) - 1
    plane_part, line_part = stencil_matrices(planes, rows_y, rows_z)
    cells_xy = planes * rows_y
    groups, packs = orbitals // GROUP, orbitals // PACK
    nb, nd = ny * nzh, nzl * nx * 2
    places, levels = nx * ny, nzl * nzh
    part, size = cells_xy // nb, nb * orbitals
    piece = size // 2 // places
    dma = pltpu.SemaphoreType.DMA
    f32, bf16 = jnp.float32, jnp.bfloat16
    hbm = pl.BlockSpec(memory_space=pltpu.HBM)
    wide = pltpu.VMEM((orbitals, planes + 2 * reach, rows_y, rows_z), bf16)
    edge = dma((STEPS, groups))
    return pl.pallas_call(
        functools.partial(step_kernel, nx, ny, nzl, nzh, float(cells_xy * rows_z * nd)),
        out_shape=jax.ShapeDtypeStruct((cells_xy, orbitals, rows_z), bf16),
        in_specs=[hbm] * 5,
        out_specs=pl.BlockSpec(memory_space=pltpu.VMEM),
        scratch_shapes=[
            pltpu.VMEM(orbital_block.shape, bf16),
            pltpu.VMEM(block_scale.shape[::-1], f32),
            pltpu.VMEM((planes, orbitals, rows_z), f32),
            pltpu.VMEM(potential.shape, f32),
            pltpu.VMEM(plane_part.shape, bf16),
            pltpu.VMEM(line_part.shape, bf16),
            wide, wide, wide,
            pltpu.VMEM((PACK, cells_xy, rows_z), f32),
            pltpu.VMEM((packs, cells_xy, PACK, rows_z), bf16),
            pltpu.VMEM((nb * packs, part * nzh, PACK, rows_z), bf16),
            pltpu.VMEM((STEPS, cells_xy, rows_z), f32),
            pltpu.VMEM((size, size), f32),
            pltpu.VMEM((size // 2, size), f32),
            pltpu.VMEM((places, piece, size), f32),
            pltpu.VMEM((levels, piece, size), f32),
            pltpu.VMEM((piece, size), f32),
            pltpu.VMEM((size, size), f32),
            pltpu.VMEM((size, size), bf16),
            pltpu.VMEM((ny * orbitals, size), bf16),
            pltpu.VMEM((ny, part * nzh, orbitals, rows_z), bf16),
            dma((groups,)), dma((4,)), edge, edge, edge, edge, dma((packs, nb)), dma((packs, nb)),
            dma, dma, dma((places,)), dma((places,)), dma((levels,)), dma((levels,)),
            dma((places,)), dma((places,)), dma, dma, dma((CHUNKS, ny)), dma((CHUNKS, ny)),
            dma((CHUNKS // nzh, ny)), dma((CHUNKS // nzh, ny)),
        ],
        compiler_params=pltpu.CompilerParams(collective_id=1, has_side_effects=True, vmem_limit_bytes=56 << 20),
        name="filter_and_rotate",
    )(orbital_block, block_scale.T, potential, jnp.asarray(plane_part), jnp.asarray(line_part))


def solution(mesh):
    nzh, nzl, nx = 2, 4, 4
    ny = mesh.shape["band"] // nzh

    def body(orbital_block, block_scale, potential):
        back = fused_step(orbital_block, block_scale, potential, nx, ny, nzl, nzh)
        return back.transpose(1, 0, 2).reshape(orbital_block.shape)

    in_specs = (P("band", "domain", None, None), P("band", "domain"), P("domain", None, None))
    out_specs = P("band", "domain", None, None)
    return jax.shard_map(body, mesh=mesh, in_specs=in_specs, out_specs=out_specs, check_vma=False)
```

```python
import functools

import jax
import jax.numpy as jnp
import ml_dtypes
import numpy as np
from jax import lax
from jax.experimental import pallas as pl
from jax.experimental.pallas import tpu as pltpu
from jax.sharding import PartitionSpec as P

MESH = pl.DeviceIdType.MESH

grid_step = 0.5
stencil_coef = (
    -5369.0 / 1800.0,
    12.0 / 7.0,
    -15.0 / 56.0,
    10.0 / 189.0,
    -1.0 / 112.0,
    2.0 / 1925.0,
    -1.0 / 16632.0,
)
lower_end = -4.0
cut_energy = 6.0
upper_end = 43.0


def filter_terms():
    width_e = (upper_end - cut_energy) / 2.0
    centre = (upper_end + cut_energy) / 2.0
    sigma_one = width_e / (lower_end - centre)
    gamma_term = 2.0 / sigma_one
    sigma_two = 1.0 / (gamma_term - sigma_one)
    sigma_three = 1.0 / (gamma_term - sigma_two)
    return (width_e, centre, sigma_one, sigma_two, sigma_three)


def remote(src, dst, send_sem, recv_sem, device):
    return pltpu.make_async_remote_copy(
        src_ref=src, dst_ref=dst, send_sem=send_sem, recv_sem=recv_sem,
        device_id=device, device_id_type=MESH,
    )


def stencil_matrices(planes, rows_y, rows_z):
    reach = len(stencil_coef) - 1
    plane_part = np.zeros((planes, rows_y, planes + 2 * reach, rows_y), np.float64)
    line_part = np.zeros((2, rows_z, 2, rows_z), np.float64)
    for m in range(1, reach + 1):
        weight = stencil_coef[m] / stencil_coef[1]
        for sign in (-m, m):
            for x in range(planes):
                for y in range(rows_y):
                    plane_part[x, y, x + reach + sign, y] += weight
                    if 0 <= y + sign < rows_y:
                        plane_part[x, y, x + reach, y + sign] += weight
            for z in range(rows_z):
                if 0 <= z + sign < rows_z:
                    for q in range(2):
                        line_part[q, z + sign, q, z] += weight
    plane_part = plane_part.reshape(planes * rows_y, (planes + 2 * reach) * rows_y)
    line_part = line_part.reshape(2 * rows_z, 2 * rows_z)
    return plane_part.astype(ml_dtypes.bfloat16), line_part.astype(ml_dtypes.bfloat16)


GROUP = 4
PACK = 8
LAG = 3
STEPS = 3
CHUNKS = 12
UNROLL = True
AHEAD = 0
EARLY = 8
PANEL = 32


def step_kernel(
    nx, ny, nzl, nzh, cells,
    orb_hbm, scale_hbm, pot_hbm, plane_hbm, line_hbm, out_ref,
    orb, scale, spread_scale, pot, plane_mat, line_mat, ext0, ext1, ext2, full, turned, cols, energy,
    gram, half, rows, line, mine, work, rot, rot_own, mixed,
    load_s, const_s, up_s, up_r, down_s, down_r, share_s, share_r,
    core_s, core_r, plane_s, plane_r, line_s, line_r, back_s, back_r, last_s, last_r, home_s, home_r, ahead_s, ahead_r,
):
    nb, nd = ny * nzh, nzl * nx * 2
    band = lax.axis_index("band")
    domain = lax.axis_index("domain")
    orbitals, planes, rows_y, rows_z = orb.shape
    reach = len(stencil_coef) - 1
    cells_xy = planes * rows_y
    part = cells_xy // nb
    groups = orbitals // GROUP
    packs = orbitals // PACK
    ext = (ext0, ext1, ext2)
    has_low, has_high = domain > 0, domain < nd - 1
    width_e, centre, sigma_one, sigma_two, sigma_three = filter_terms()
    kinetic = -0.5 / (grid_step * grid_step)

    y, z_hi = band // nzh, lax.rem(band, nzh)
    core = lax.rem(domain, 2)
    x = lax.rem(domain // 2, nx)
    z_lo = domain // (2 * nx)
    place = y * nx + x
    places = nx * ny
    level = z_hi * nzl + z_lo
    levels = nzl * nzh
    partner = (band, domain + 1 - 2 * core)

    def at_place(p):
        return ((p // nx) * nzh + z_hi, (z_lo * nx + lax.rem(p, nx)) * 2 + core)

    def at_level(l):
        return (y * nzh + l // nzl, (lax.rem(l, nzl) * nx + x) * 2 + core)

    def load(g):
        some = pl.ds(g * GROUP, GROUP)
        return pltpu.make_async_copy(orb_hbm.at[some], orb.at[some], load_s.at[g])

    constants = [
        pltpu.make_async_copy(source, target, const_s.at[i])
        for i, (source, target) in enumerate(((scale_hbm, scale), (pot_hbm, pot), (plane_hbm, plane_mat), (line_hbm, line_mat)))
    ]
    constants[0].start()
    load(0).start()
    for copy in constants[1:]:
        copy.start()
    for g in range(1, groups):
        load(g).start()

    barrier = pltpu.get_barrier_semaphore()

    def greet(device):
        pl.semaphore_signal(barrier, inc=1, device_id=device, device_id_type=MESH)

    @pl.when(has_low)
    def _():
        greet((band, domain - 1))

    @pl.when(has_high)
    def _():
        greet((band, domain + 1))

    for k in range(1, nb):
        greet((lax.rem(band + k, nb), domain))
    greet(partner)
    for k in range(1, places):
        greet(at_place(lax.rem(place + k, places)))
    for k in range(1, levels):
        greet(at_level(lax.rem(level + k, levels)))

    def scale_group(g):
        load(g).wait()

        def one(i, carry):
            o = g * GROUP + i
            for p in range(planes):
                ext0[o, reach + p] = (orb[o, p].astype(jnp.float32) * spread_scale[p, pl.ds(o, 1), :]).astype(jnp.bfloat16)
            return carry

        lax.fori_loop(0, GROUP, one, 0)

    def upward(s, g):
        some = pl.ds(g * GROUP, GROUP)
        return remote(ext[s].at[some, pl.ds(planes, reach)], ext[s].at[some, pl.ds(0, reach)],
                      up_s.at[s, g], up_r.at[s, g], (band, domain + 1))

    def downward(s, g):
        some = pl.ds(g * GROUP, GROUP)
        return remote(ext[s].at[some, pl.ds(reach, reach)], ext[s].at[some, pl.ds(planes + reach, reach)],
                      down_s.at[s, g], down_r.at[s, g], (band, domain - 1))

    def send_edges(s, g):
        @pl.when(has_high)
        def _():
            upward(s, g).start()

        @pl.when(has_low)
        def _():
            downward(s, g).start()

    def await_edges(s, g):
        @pl.when(has_low)
        def _():
            upward(s, g).wait_recv()

        @pl.when(has_high)
        def _():
            downward(s, g).wait_recv()

    outer = (sigma_one / width_e, 2.0 * sigma_two / width_e, 2.0 * sigma_three / width_e)
    inner = (None, sigma_one * sigma_two, sigma_two * sigma_three)

    def apply(s, g):
        def pair(i, carry):
            o = g * GROUP + 2 * i
            sources = [ext[s][o + q].reshape((planes + 2 * reach) * rows_y, rows_z) for q in range(2)]
            both = jnp.concatenate(sources, axis=1)
            middle = both[reach * rows_y : reach * rows_y + cells_xy]
            spread = jnp.dot(plane_mat[...], both, preferred_element_type=jnp.float32)
            spread = spread + jnp.dot(middle, line_mat[...], preferred_element_type=jnp.float32)
            for q in range(2):
                lanes = slice(q * rows_z, (q + 1) * rows_z)
                value = spread[:, lanes] * (outer[s] * kinetic * stencil_coef[1])
                value = value + energy[s] * middle[:, lanes].astype(jnp.float32)
                if s > 0:
                    earlier = ext[s - 1][o + q, pl.ds(reach, planes)].reshape(cells_xy, rows_z)
                    value = value - inner[s] * earlier.astype(jnp.float32)
                if s < STEPS - 1:
                    ext[s + 1][o + q, pl.ds(reach, planes)] = value.astype(jnp.bfloat16).reshape(planes, rows_y, rows_z)
                else:
                    full[lax.rem(o, PACK) + q] = value
            return carry

        lax.fori_loop(0, GROUP // 2, pair, 0, unroll=UNROLL)

    def turn(h):
        def block(r, carry):
            at = pl.multiple_of(r * 8, 8)
            piece = full[:, pl.ds(at, 8), :]
            turned[h, pl.ds(at, 8)] = jnp.swapaxes(piece, 0, 1).astype(jnp.bfloat16)
            return carry

        lax.fori_loop(0, cells_xy // 8, block, 0)

    span_rows = part * nzh
    my_rows = pl.ds(pl.multiple_of(z_hi * part, 8), part)

    def same_share(h, k):
        target = lax.rem(y + k, ny)
        return remote(turned.at[h, pl.ds(target * span_rows, span_rows)], cols.at[band * packs + h],
                      share_s.at[h, k], share_r.at[h, k], (target * nzh + z_hi, domain))

    def cross_share(h, k):
        target = lax.rem(y + k, ny)
        there = 1 - z_hi
        rows_there = pl.ds(pl.multiple_of(there * part, 8), part)
        return remote(turned.at[h, pl.ds(pl.multiple_of((target * nzh + there) * part, 8), part)],
                      cols.at[band * packs + h, rows_there],
                      share_s.at[h, ny + k], share_r.at[h, ny + k], (target * nzh + there, domain))

    def shares(h):
        return [cross_share(h, k) for k in range(ny)] + [same_share(h, k) for k in range(1, ny)]

    rows_each = span_rows // CHUNKS
    blocks = part // rows_each
    opposite = (y * nzh + 1 - z_hi, domain)

    def ahead(i, k):
        rows_i = pl.ds(pl.multiple_of(z_hi * part + i * rows_each, 2), rows_each)
        block = cols.at[pl.ds((k * nzh + z_hi) * packs, packs), rows_i]
        return remote(block, block, ahead_s.at[i, k], ahead_r.at[i, k], opposite)

    def ahead_start(i):
        for k in range(ny - 1):
            ahead(i, k).start()

        @pl.when(z_hi == 0)
        def _():
            ahead(i, ny - 1).start()

    def ahead_wait(i):
        for k in range(ny - 1):
            ahead(i, k).wait()

        @pl.when(z_hi == 0)
        def _():
            ahead(i, ny - 1).wait_send()

        @pl.when(z_hi == 1)
        def _():
            ahead(i, ny - 1).wait_recv()

    constants[0].wait()
    upright = scale[...].T
    for p in range(planes):
        spread_scale[p] = jnp.broadcast_to(upright[:, p : p + 1], (orbitals, rows_z))
    for g in range(EARLY):
        scale_group(g)
    constants[1].wait()
    shifted = pot[...].reshape(cells_xy, rows_z) + (3.0 * stencil_coef[0] * kinetic - centre)
    for s in range(STEPS):
        energy[s] = shifted * outer[s]
    pl.semaphore_wait(
        barrier, nb - 1 + places + levels - 1 + has_low.astype(jnp.int32) + has_high.astype(jnp.int32)
    )
    for g in range(LAG + 1):
        send_edges(0, g)

    @pl.when(jnp.logical_not(has_low))
    def _():
        for s in range(STEPS):
            ext[s][:, :reach] = jnp.zeros((orbitals, reach, rows_y, rows_z), jnp.bfloat16)

    @pl.when(jnp.logical_not(has_high))
    def _():
        for s in range(STEPS):
            ext[s][:, planes + reach :] = jnp.zeros((orbitals, reach, rows_y, rows_z), jnp.bfloat16)

    for copy in constants[2:]:
        copy.wait()

    for t in range(groups + (STEPS - 1) * LAG):
        for s in range(STEPS):
            g = t - s * LAG
            if not 0 <= g < groups:
                continue
            await_edges(s, g)
            apply(s, g)
            if s < STEPS - 1:
                send_edges(s + 1, g)
            if s == 0 and g + LAG + 1 < groups:
                if g + LAG + 1 >= EARLY:
                    scale_group(g + LAG + 1)
                send_edges(0, g + LAG + 1)
            if s == STEPS - 1 and (g + 1) * GROUP % PACK == 0:
                h = g * GROUP // PACK
                turn(h)
                for copy in shares(h):
                    copy.start()
                cols[band * packs + h] = turned[h, pl.ds(y * span_rows, span_rows)]

    for h in range(packs):
        for copy in shares(h):
            copy.wait()
    for i in range(AHEAD):
        ahead_start(i)

    @pl.when(z_hi == 0)
    def _():
        cols[pl.ds((nb - 1) * packs, packs), pl.ds(part, part)] = jnp.zeros((packs, part, PACK, rows_z), jnp.bfloat16)


    total_orbitals = nb * orbitals

    def column(r):
        return cols[:, r].reshape(total_orbitals, rows_z)

    def gram_step(i, total):
        r = z_hi * part + 2 * i
        both = jnp.concatenate([column(r), column(r + 1)], axis=1)
        return total + lax.dot_general(both, both, (((1,), (1,)), ((), ())), preferred_element_type=jnp.float32)

    gram[...] = lax.fori_loop(0, part // 2, gram_step, jnp.zeros(gram.shape, jnp.float32))

    half_rows = total_orbitals // 2
    piece = half_rows // places
    mine_at = pl.multiple_of(core * half_rows, 8)
    other_at = pl.multiple_of((1 - core) * half_rows, 8)
    swap = remote(gram.at[pl.ds(other_at, half_rows)], half, core_s, core_r, partner)
    swap.start()
    swap.wait()
    half[...] += gram[pl.ds(mine_at, half_rows), :]

    copies = []
    for k in range(1, places):
        p = lax.rem(place + k, places)
        copy = remote(half.at[pl.ds(pl.multiple_of(p * piece, 8), piece)], rows.at[place],
                      plane_s.at[k], plane_r.at[k], at_place(p))
        copy.start()
        copies.append(copy)
    rows[place] = half[pl.ds(pl.multiple_of(place * piece, 8), piece), :]
    for copy in copies:
        copy.wait()
    total = rows[0]
    for k in range(1, places):
        total = total + rows[k]
    mine[...] = total

    copies = []
    for k in range(1, levels):
        l = lax.rem(level + k, levels)
        copy = remote(mine, line.at[level], line_s.at[k], line_r.at[k], at_level(l))
        copy.start()
        copies.append(copy)
    line[level] = mine[...]
    for copy in copies:
        copy.wait()
    for i in range(AHEAD, blocks):
        ahead_start(i)
    total = line[0]
    for k in range(1, levels):
        total = total + line[k]
    own = pl.ds(pl.multiple_of(mine_at + place * piece, 8), piece)
    work[own, :] = total

    copies = []
    for k in range(1, places):
        p = lax.rem(place + k, places)
        copy = remote(work.at[own], work.at[own], back_s.at[k], back_r.at[k], at_place(p))
        copy.start()
        copies.append(copy)
    for copy in copies:
        copy.wait()
    span = pl.ds(mine_at, half_rows)
    final = remote(work.at[span], work.at[span], last_s, last_r, partner)
    final.start()
    final.wait()

    factor_inverse(cells, work, rot)

    for k in range(ny):
        rot_own[pl.ds(k * orbitals, orbitals), :] = rot[pl.ds(pl.multiple_of((k * nzh + z_hi) * orbitals, orbitals), orbitals), :]
    def chunk_row(c):
        return pl.multiple_of(lax.rem(z_hi * part + c * rows_each, span_rows), 2)

    def home(c, k):
        target = lax.rem(y + k, ny)
        first = chunk_row(c)
        return remote(mixed.at[target, pl.ds(first, rows_each)],
                      out_ref.at[pl.ds(y * span_rows + first, rows_each)],
                      home_s.at[c, k], home_r.at[c, k], (target * nzh + z_hi, domain))

    for c in range(CHUNKS):
        if c >= blocks:
            ahead_wait(c - blocks)

        def mix(i, carry):
            r = chunk_row(c) + 2 * i
            both = jnp.concatenate([column(r), column(r + 1)], axis=1)
            value = jnp.dot(rot_own[...], both, preferred_element_type=jnp.float32).astype(jnp.bfloat16)
            mixed[:, r] = value[:, :rows_z].reshape(ny, orbitals, rows_z)
            mixed[:, r + 1] = value[:, rows_z:].reshape(ny, orbitals, rows_z)
            return carry

        lax.fori_loop(0, rows_each // 2, mix, 0)
        for k in range(1, ny):
            home(c, k).start()

    out_ref[pl.ds(y * span_rows, span_rows)] = mixed[y]
    for c in range(CHUNKS):
        for k in range(1, ny):
            home(c, k).wait()
    for s in range(STEPS):
        for g in range(groups):
            @pl.when(has_high)
            def _():
                upward(s, g).wait_send()

            @pl.when(has_low)
            def _():
                downward(s, g).wait_send()


def factor_inverse(cells, work, out_ref):
    size = work.shape[0]
    panel = PANEL
    work[...] = work[...] * (1.0 / cells)
    lane = lax.broadcasted_iota(jnp.int32, (panel, size), 1)
    row = lax.broadcasted_iota(jnp.int32, (panel, size), 0)
    sub = lax.broadcasted_iota(jnp.int32, (panel, 128), 0)
    wide = lax.broadcasted_iota(jnp.int32, (size, size), 1)

    def step(k, carry):
        start = pl.multiple_of(k * panel, panel)
        tile = pl.multiple_of((start // 128) * 128, 128)
        here = pl.ds(start, panel)
        corner = pltpu.roll(work[here, pl.ds(tile, 128)], 128 - (start - tile), 1)
        rows = work[here, :]
        inside = (lane >= start) & (lane < start + panel)
        rows = jnp.where(inside, jnp.where(lane - start == row, 1.0, 0.0), rows)
        columns = [jnp.broadcast_to(corner[:, j : j + 1], (panel, 128)) for j in range(panel)]
        pivots = jnp.ones((panel, 128), jnp.float32)
        for j in range(panel):
            spread = [jnp.broadcast_to(columns[j][l : l + 1, :], (panel, 128)) for l in range(j, panel)]
            pivot = spread[0]
            pivots = jnp.where(sub == j, pivot, pivots)
            if j < panel - 1:
                factor = jnp.where(sub > j, columns[j] * (1.0 / pivot), 0.0)
                for l in range(j + 1, panel):
                    columns[l] = columns[l] - factor * spread[l - j]
                wide_factor = jnp.concatenate([factor] * (size // 128), axis=1)
                rows = rows - wide_factor * jnp.broadcast_to(rows[j : j + 1, :], (panel, size))
        scale = lax.rsqrt(pivots)
        rows = rows * jnp.concatenate([scale] * (size // 128), axis=1)
        below = jnp.where(lane >= start + panel, rows, 0.0)
        change = lax.dot_general(
            below, rows, (((0,), (0,)), ((), ())),
            precision=lax.Precision.HIGHEST, preferred_element_type=jnp.float32,
        )
        keep = (wide >= start) & (wide < start + panel)
        work[...] = jnp.where(keep, 0.0, work[...]) - change
        work[here, :] = rows
        return carry

    lax.fori_loop(0, size // panel, step, 0)
    down = lax.broadcasted_iota(jnp.int32, (size, size), 0)
    out_ref[...] = jnp.where(wide <= down, work[...], 0.0).astype(out_ref.dtype)


def fused_step(orbital_block, block_scale, potential, nx, ny, nzl, nzh):
    orbitals, planes, rows_y, rows_z = orbital_block.shape
    reach = len(stencil_coef) - 1
    plane_part, line_part = stencil_matrices(planes, rows_y, rows_z)
    cells_xy = planes * rows_y
    groups, packs = orbitals // GROUP, orbitals // PACK
    nb, nd = ny * nzh, nzl * nx * 2
    places, levels = nx * ny, nzl * nzh
    part, size = cells_xy // nb, nb * orbitals
    piece = size // 2 // places
    dma = pltpu.SemaphoreType.DMA
    f32, bf16 = jnp.float32, jnp.bfloat16
    hbm = pl.BlockSpec(memory_space=pltpu.HBM)
    wide = pltpu.VMEM((orbitals, planes + 2 * reach, rows_y, rows_z), bf16)
    edge = dma((STEPS, groups))
    return pl.pallas_call(
        functools.partial(step_kernel, nx, ny, nzl, nzh, float(cells_xy * rows_z * nd)),
        out_shape=jax.ShapeDtypeStruct((cells_xy, orbitals, rows_z), bf16),
        in_specs=[hbm] * 5,
        out_specs=pl.BlockSpec(memory_space=pltpu.VMEM),
        scratch_shapes=[
            pltpu.VMEM(orbital_block.shape, bf16),
            pltpu.VMEM(block_scale.shape[::-1], f32),
            pltpu.VMEM((planes, orbitals, rows_z), f32),
            pltpu.VMEM(potential.shape, f32),
            pltpu.VMEM(plane_part.shape, bf16),
            pltpu.VMEM(line_part.shape, bf16),
            wide, wide, wide,
            pltpu.VMEM((PACK, cells_xy, rows_z), f32),
            pltpu.VMEM((packs, cells_xy, PACK, rows_z), bf16),
            pltpu.VMEM((nb * packs, part * nzh, PACK, rows_z), bf16),
            pltpu.VMEM((STEPS, cells_xy, rows_z), f32),
            pltpu.VMEM((size, size), f32),
            pltpu.VMEM((size // 2, size), f32),
            pltpu.VMEM((places, piece, size), f32),
            pltpu.VMEM((levels, piece, size), f32),
            pltpu.VMEM((piece, size), f32),
            pltpu.VMEM((size, size), f32),
            pltpu.VMEM((size, size), bf16),
            pltpu.VMEM((ny * orbitals, size), bf16),
            pltpu.VMEM((ny, part * nzh, orbitals, rows_z), bf16),
            dma((groups,)), dma((4,)), edge, edge, edge, edge, dma((packs, nb)), dma((packs, nb)),
            dma, dma, dma((places,)), dma((places,)), dma((levels,)), dma((levels,)),
            dma((places,)), dma((places,)), dma, dma, dma((CHUNKS, ny)), dma((CHUNKS, ny)),
            dma((CHUNKS // nzh, ny)), dma((CHUNKS // nzh, ny)),
        ],
        compiler_params=pltpu.CompilerParams(collective_id=1, has_side_effects=True, vmem_limit_bytes=56 << 20),
        name="filter_and_rotate",
    )(orbital_block, block_scale.T, potential, jnp.asarray(plane_part), jnp.asarray(line_part))


def solution(mesh):
    nzh, nzl, nx = 2, 4, 4
    ny = mesh.shape["band"] // nzh

    def body(orbital_block, block_scale, potential):
        back = fused_step(orbital_block, block_scale, potential, nx, ny, nzl, nzh)
        return back.transpose(1, 0, 2).reshape(orbital_block.shape)

    in_specs = (P("band", "domain", None, None), P("band", "domain"), P("domain", None, None))
    out_specs = P("band", "domain", None, None)
    return jax.shard_map(body, mesh=mesh, in_specs=in_specs, out_specs=out_specs, check_vma=False)
```
